32 devices in a mesh: member: 2 (over y), lon: 8 (over z, x), lat: 2 (over core).
Axes of the slice: x: 2, y: 2, z: 4, core: 2. Of those that a mesh axis runs over, the one named last changes fastest.
Arguments:
- fields: bfloat16 [1280, 32, 128], P('member', 'lat', 'lon'), parts along dimension 0, may hold values from -6 to 6
- support_rows: int32 [7, 32, 16], replicated, may hold values from -1 to 1
- support_lons: int32 [7, 32, 16], replicated, may hold values from -64 to 64, as said below
- support_weights: float32 [7, 32, 16], replicated, may hold values from -1.5 to 1.5
- mix_weight: bfloat16 [7, 640, 640], replicated, may hold values from -0.09375 to 0.09375
- norm_gain: float32 [640], replicated, may hold values from 0.1 to 1.9
- up_weight: bfloat16 [640, 1280], replicated, may hold values from -0.25 to 0.25
- down_weight: bfloat16 [1280, 640], replicated, may hold values from -0.15625 to 0.15625
Outputs:
- output: bfloat16 [1280, 32, 128], P('member', 'lat', 'lon'), parts along dimension 0
The draws below stay inside these ranges and needn't reach their ends.
There are 2 independent parts, one for each index of `member`. The reference program is written for one: setup_inputs(seed, part) draws one part's arguments, and reference() takes and returns one part's arrays. A program takes and returns all parts, laid end to end along the dimension named above; an argument that names none is the same for every part. Nothing has to cross between parts.
Inputs may be any that keep to these rules, and one draw needn't show every extreme that they name: `support_lons`: at output row i every offset lies within plus or minus min(64, 4 * 32 // min(i + 1, 32 - i)); in every basis filter the first pole row has an entry at -(64) and the last pole row one at 64.
All inputs are finite; a program needn't handle non-finite values.
Results may differ from the reference program's by a relative error of at most 0.0095.
Values may be sent and summed in bfloat16 or wider, within the bound.
No kernel may reach another device: no remote copies, remote signals or barrier semaphores. Data moves between devices by JAX's collectives and lax.ppermute only.
A program may use at most 128 MiB of HBM per device.

```python
import math
import jax
import jax.numpy as jnp
from jax import lax

C = 640
HID = 1280
K = 7
S = 16
NLAT = 32
NLON = 128


def draw_support_rows(key, part):
    return jax.random.randint(key, (K, NLAT, S), -1, 2, dtype=jnp.int32)


def draw_support_lons(key, part):
    row_index = lax.broadcasted_iota(jnp.int32, (K, NLAT, S), 1)
    slot_index = lax.broadcasted_iota(jnp.int32, (K, NLAT, S), 2)
    nearest = jnp.minimum(row_index + 1, NLAT - row_index)
    half_reach = jnp.minimum(NLON // 2, 4 * NLAT // nearest)
    random_bits = jax.random.randint(key, (K, NLAT, S), 0, 2 ** 30, dtype=jnp.int32)
    offset = jnp.mod(random_bits, 2 * half_reach + 1) - half_reach
    offset = jnp.where((row_index == 0) & (slot_index == 0), -(NLON // 2), offset)
    offset = jnp.where((row_index == NLAT - 1) & (slot_index == 0), NLON // 2, offset)
    return offset.astype(jnp.int32)


def block_levels(rng, extent, shards, smallest, largest):
    loudness, own = 1.0, jax.random.fold_in(rng, 6)
    for dim, shards_of in shards:
        heights = jnp.exp(jax.random.uniform(jax.random.fold_in(own, dim), (shards_of,), jnp.float32, smallest / len(shards), largest / len(shards)))
        loudness = loudness * jnp.repeat(heights, extent[dim] // shards_of).reshape([-1 if axis == dim else 1 for axis in range(len(extent))])
    return loudness


def bell_draw(key, shape, width, reach, split=(), kind=jnp.bfloat16):
    drawn = jax.random.normal(key, shape, jnp.float32) * width
    if len(split) > 0:
        drawn = block_levels(key, shape, split, -0.22, 0.18) * drawn
    return jnp.clip(drawn, min=-reach, max=reach).astype(kind)


def setup_inputs(seed: int = 0, part: int = 0) -> dict:
    seeds = jax.random.split(jax.random.key(seed), 9)
    part_keys = jax.random.split(jax.random.fold_in(seeds[8], part), 9)
    return {
        "fields": bell_draw(part_keys[0], (C, NLAT, NLON), 1.0, 6.0, ((1, 2), (2, 8))),
        "support_rows": draw_support_rows(jax.random.fold_in(seeds[8], 71), part),
        "support_lons": draw_support_lons(jax.random.fold_in(seeds[8], 71), part),
        "support_weights": bell_draw(seeds[3], (K, NLAT, S), 0.25, 1.5, (), jnp.float32),
        "mix_weight": bell_draw(seeds[4], (K, C, C), (K * C) ** -0.5, 0.09375),
        "norm_gain": jnp.clip(1.0 + 0.18 * jax.random.normal(seeds[5], (C,), jnp.float32), 0.1, 1.9),
        "up_weight": bell_draw(seeds[6], (C, HID), C ** -0.5, 0.25),
        "down_weight": bell_draw(seeds[7], (HID, C), HID ** -0.5, 0.15625),
    }


full_turn = 2.0 * math.pi
norm_eps = 1e-05

def round_half(values):
    return lax.optimization_barrier(values.astype(jnp.bfloat16)).astype(jnp.float32)

def reference(fields, support_rows, support_lons, support_weights, mix_weight, norm_gain, up_weight, down_weight):
    lon_total = NLON
    lon_half = lon_total // 2
    frequency = jnp.arange(lon_half + 1, dtype=jnp.int32)
    spectrum = jnp.fft.rfft(fields.astype(jnp.float32), axis=2)
    cos_part = jnp.pad(round_half(jnp.real(spectrum).astype(jnp.float32)), ((0, 0), (1, 1), (0, 0)))
    sin_part = jnp.pad(round_half((-jnp.imag(spectrum)).astype(jnp.float32)), ((0, 0), (1, 1), (0, 0)))

    def basis_term(running, basis_index):
        row_offsets = support_rows[basis_index]
        lon_offsets = support_lons[basis_index]
        weights = support_weights[basis_index]
        turns = jnp.mod(lon_offsets[:, :, None] * frequency[None, None, :], lon_total).astype(jnp.int32)
        phase_angle = turns.astype(jnp.float32) * (full_turn / lon_total)
        cos_table = jnp.cos(phase_angle)
        sin_table = jnp.sin(phase_angle)
        spec_cos = jnp.zeros((C, NLAT, lon_half + 1), jnp.float32)
        spec_sin = jnp.zeros((C, NLAT, lon_half + 1), jnp.float32)
        for offset in (-1, 0, 1):
            picked = jnp.where(row_offsets == offset, weights, jnp.zeros_like(weights))
            filter_cos = jnp.einsum('is,isf->if', picked, cos_table, precision=lax.Precision.HIGHEST)
            filter_sin = jnp.einsum('is,isf->if', picked, sin_table, precision=lax.Precision.HIGHEST)
            field_cos = cos_part[:, 1 + offset:1 + offset + NLAT]
            field_sin = sin_part[:, 1 + offset:1 + offset + NLAT]
            spec_cos = spec_cos + field_cos * filter_cos + field_sin * filter_sin
            spec_sin = spec_sin + field_sin * filter_cos - field_cos * filter_sin
        weight_k = mix_weight[basis_index]
        run_cos = running[0] + lax.dot_general(weight_k, spec_cos.astype(jnp.bfloat16).reshape(C, -1), (((0,), (0,)), ((), ())), preferred_element_type=jnp.float32)
        run_sin = running[1] + lax.dot_general(weight_k, spec_sin.astype(jnp.bfloat16).reshape(C, -1), (((0,), (0,)), ((), ())), preferred_element_type=jnp.float32)
        return ((run_cos, run_sin), None)
    start = jnp.zeros((C, NLAT * (lon_half + 1)), jnp.float32)
    mixed_parts, _ = lax.scan(basis_term, (start, start), jnp.arange(K, dtype=jnp.int32))
    mixed_cos = mixed_parts[0].reshape(C, NLAT, lon_half + 1)
    mixed_sin = mixed_parts[1].reshape(C, NLAT, lon_half + 1)
    mixed = jnp.fft.irfft(lax.complex(mixed_cos, -mixed_sin), n=lon_total, axis=2).astype(jnp.float32)
    latent = fields.reshape(C, NLAT * NLON).astype(jnp.float32) + mixed.reshape(C, NLAT * NLON)
    row_mean = lax.optimization_barrier(jnp.mean(latent, axis=0))
    variance = lax.optimization_barrier(jnp.mean(jnp.square(latent - row_mean), axis=0))
    normed = ((latent - row_mean) * lax.rsqrt(variance + norm_eps) * norm_gain[:, None]).astype(jnp.bfloat16)
    hidden = jax.nn.gelu(lax.dot_general(up_weight, normed, (((0,), (0,)), ((), ())), preferred_element_type=jnp.float32), approximate=False).astype(jnp.bfloat16)
    output = latent + lax.dot_general(down_weight, hidden, (((0,), (0,)), ((), ())), preferred_element_type=jnp.float32)
    return output.astype(jnp.bfloat16).reshape(C, NLAT, NLON)
```

```python
import math

import jax
import jax.numpy as jnp
from jax import lax
from jax.sharding import PartitionSpec as P

norm_eps = 1e-05


def reach_of(row, lat_total, lon_total):
    return min(lon_total // 2, 4 * lat_total // min(row + 1, lat_total - row))


def needed_columns(rows, lat_shards, lat_total, lon_total):
    need = [0] * (rows + 2)
    for shard in range(lat_shards // 2):
        for slot in range(rows):
            reach = reach_of(shard * rows + slot, lat_total, lon_total)
            for source in (slot, slot + 1, slot + 2):
                if shard == 0 and source == 0:
                    continue
                need[source] = max(need[source], reach)
    return need


def on_device(
    fields,
    support_rows,
    support_lons,
    support_weights,
    mix_weight,
    norm_gain,
    up_weight,
    down_weight,
):
    channels, rows, cols = fields.shape
    kinds, lat_total, entries = support_rows.shape
    lon_shards = lax.axis_size("lon")
    lat_shards = lax.axis_size("lat")
    lon_total = lon_shards * cols
    need = needed_columns(rows, lat_shards, lat_total, lon_total)
    lat = lax.axis_index("lat")
    south = lat >= lat_shards // 2
    x = jnp.transpose(fields, (1, 2, 0))
    forward = [(i, i + 1) for i in range(lat_shards - 1)]
    backward = [(b, a) for a, b in forward]
    low = lax.ppermute(x[rows - 1 :], "lat", forward)
    high = lax.ppermute(x[:1], "lat", backward)
    x = jnp.concatenate([low, x, high], axis=0)
    x = jnp.where(south, x[::-1], x)
    half = lon_shards // 2
    window = {0: x}
    for dist in range(1, half + 1):
        for sign in (1, -1):
            if dist == half and sign == -1:
                continue
            widths = []
            for slot in range(rows + 2):
                width = max(0, min(cols, need[slot] - (dist - 1) * cols))
                if dist == half and width > 0:
                    width = cols
                widths.append(width)
            picks = [(slot, width) for slot, width in enumerate(widths) if width > 0]
            if not picks:
                continue
            pieces = [
                x[slot, :width] if sign == 1 else x[slot, cols - width :] for slot, width in picks
            ]
            sent = jnp.concatenate(pieces, axis=0)
            got = lax.ppermute(
                sent, "lon", [((i + sign * dist) % lon_shards, i) for i in range(lon_shards)]
            )
            blocks = []
            start = 0
            for slot, width in enumerate(widths):
                piece = got[start : start + width]
                start += width
                gap = jnp.zeros((cols - width, channels), x.dtype)
                blocks.append(
                    jnp.concatenate([piece, gap] if sign == 1 else [gap, piece], axis=0)
                )
            window[(sign * dist) % lon_shards] = jnp.stack(blocks)
    empty = jnp.zeros_like(x)
    wide = jnp.concatenate([window.get(b, empty) for b in range(lon_shards)], axis=1)

    row_start = lat * rows
    row_sel = lax.dynamic_slice_in_dim(support_rows, row_start, rows, 1)
    lon_sel = lax.dynamic_slice_in_dim(support_lons, row_start, rows, 1)
    weight_sel = lax.dynamic_slice_in_dim(support_weights, row_start, rows, 1)
    row_sel = jnp.where(south, -row_sel[:, ::-1], row_sel)
    lon_sel = jnp.where(south, lon_sel[:, ::-1], lon_sel)
    weight_sel = jnp.where(south, weight_sel[:, ::-1], weight_sel)
    place = jnp.arange(lon_total, dtype=jnp.int32)
    column = jnp.arange(cols, dtype=jnp.int32)
    response = None
    for offset in (-1, 0, 1):
        picked = jnp.where(row_sel == offset, weight_sel, 0.0)
        taps = jnp.zeros((rows, kinds, cols, lon_total), jnp.float32)
        for entry in range(entries):
            spot = jnp.mod(
                jnp.transpose(lon_sel[:, :, entry])[:, :, None] + column, lon_total
            )
            taps = taps + jnp.where(
                spot[..., None] == place,
                jnp.transpose(picked[:, :, entry])[:, :, None, None],
                0.0,
            )
        taps = taps.astype(jnp.bfloat16).reshape(rows, kinds * cols, lon_total)
        piece = lax.dot_general(
            taps,
            wide[1 + offset : 1 + offset + rows],
            (((2,), (1,)), ((0,), (0,))),
            preferred_element_type=jnp.float32,
        )
        response = piece if response is None else response + piece
    response = response.astype(jnp.bfloat16).reshape(rows, kinds, cols, channels)
    mixed = None
    for kind in range(kinds):
        piece = jnp.dot(
            response[:, kind].reshape(rows * cols, channels),
            mix_weight[kind],
            preferred_element_type=jnp.float32,
        )
        mixed = piece if mixed is None else mixed + piece
    latent = x[1 : rows + 1].reshape(rows * cols, channels).astype(jnp.float32) + mixed
    mean = jnp.mean(latent, axis=1, keepdims=True)
    variance = jnp.mean(jnp.square(latent - mean), axis=1, keepdims=True)
    normed = ((latent - mean) * lax.rsqrt(variance + norm_eps) * norm_gain).astype(jnp.bfloat16)
    hidden = jax.nn.gelu(
        jnp.dot(normed, up_weight, preferred_element_type=jnp.float32), approximate=False
    ).astype(jnp.bfloat16)
    output = latent + jnp.dot(hidden, down_weight, preferred_element_type=jnp.float32)
    output = output.astype(jnp.bfloat16).reshape(rows, cols, channels)
    output = jnp.where(south, output[::-1], output)
    return jnp.transpose(output, (2, 0, 1))


def solution(mesh):
    in_specs = (P("member", "lat", "lon"), P(), P(), P(), P(), P(), P(), P())
    out_specs = P("member", "lat", "lon")
    return jax.shard_map(
        on_device, mesh=mesh, in_specs=in_specs, out_specs=out_specs, check_vma=False
    )
```

```python
import functools

import jax
import jax.numpy as jnp
from jax import lax
from jax.experimental import pallas as pl
from jax.experimental.pallas import tpu as pltpu
from jax.sharding import PartitionSpec as P

norm_eps = 1e-05
lanes = 128
vmem = pl.BlockSpec(memory_space=pltpu.VMEM)


class Plan:
    def __init__(self, rows, cols, lat_shards, lon_shards):
        self.rows, self.cols = rows, cols
        self.lat_shards, self.lon_shards = lat_shards, lon_shards
        lat_total, lon_total = rows * lat_shards, cols * lon_shards
        self.lon_total = lon_total
        self.half = lon_shards // 2
        self.outer = lat_shards > 2
        reach = [0] * rows
        need = [0] * (rows + 2)
        for shard in range(lat_shards // 2):
            for slot in range(rows):
                row = shard * rows + slot
                span = min(lon_total // 2, 4 * lat_total // min(row + 1, lat_total - row))
                reach[slot] = max(reach[slot], span)
                for source in (slot, slot + 1, slot + 2):
                    need[source] = max(need[source], span)
        if not self.outer:
            need[0] = 0
        self.blocks = [min(self.half, -(-span // cols)) for span in reach]
        self.moves = []
        for dist in range(1, self.half + 1):
            for sign in (1, -1):
                if dist == self.half and sign == -1:
                    continue
                picks, start = [], 0
                for slot in range(rows + 2):
                    width = max(0, min(cols, need[slot] - (dist - 1) * cols))
                    if width > 0:
                        width = cols if dist == self.half else width
                        picks.append((slot, start, width))
                        start += width
                if picks:
                    self.moves.append((dist, sign, picks, start))

    def span(self, slot):
        blocks = self.blocks[slot]
        if blocks == self.half:
            return 0, self.lon_total
        return (self.half - 1 - blocks) * self.cols, (2 * blocks + 1) * self.cols

    def sources(self, slot):
        return [s for s in (slot, slot + 1, slot + 2) if s > 0 or self.outer]


def is_south(plan):
    return lax.axis_index("lat") >= plan.lat_shards // 2


def row_of(plan, south, slot):
    return jnp.where(south, plan.rows - slot, slot - 1)


def load_slot(plan, south, slot, x_ref, low_ref, high_ref):
    if slot == 0:
        return jnp.where(south, high_ref[0], low_ref[0])
    if slot == plan.rows + 1:
        return jnp.where(south, low_ref[0], high_ref[0])
    return x_ref[row_of(plan, south, slot)]


def pack_body(plan, moves, halo, *refs):
    low_ref, high_ref = refs[1:3] if halo else (None, None)
    outs = refs[3:] if halo else refs[1:]
    south = is_south(plan)
    for (_, sign, picks, _), out in zip(moves, outs):
        for slot, start, width in picks:
            block = load_slot(plan, south, slot, refs[0], low_ref, high_ref)
            block = block[:width] if sign == 1 else block[plan.cols - width :]
            out[start : start + width] = block


def pack(plan, moves, x, low, high):
    halo = low is not None
    args = (x, low, high) if halo else (x,)
    return pl.pallas_call(
        functools.partial(pack_body, plan, moves, halo),
        out_shape=[jax.ShapeDtypeStruct((m[3], x.shape[2]), x.dtype) for m in moves],
        in_specs=[vmem] * len(args),
        out_specs=[vmem] * len(moves),
        name="pack_columns",
    )(*args)


def taps_body(plan, kinds, entries, support_ref, out):
    south = is_south(plan)
    row_start = lax.axis_index("lat") * plan.rows
    width = out.shape[2]
    spot = lax.broadcasted_iota(jnp.int32, (kinds, width), 1).astype(jnp.float32)
    index = 0
    for slot in range(plan.rows):
        center = (plan.half - 1) * plan.cols - plan.span(slot)[0]
        tile = support_ref[row_start + row_of(plan, south, slot + 1)]
        lift = jnp.where(south, -tile[0], tile[0])
        place = tile[1] + center
        place = jnp.where(place < 0, place + plan.lon_total, place)
        for source in plan.sources(slot):
            weight = jnp.where(lift == (source - slot - 1), tile[2], 0.0)
            taps = jnp.zeros((kinds, width), jnp.float32)
            for entry in range(entries):
                hit = place[:, entry : entry + 1] == spot
                taps = taps + jnp.where(hit, weight[:, entry : entry + 1], 0.0)
            for kind in range(kinds):
                spread = jnp.broadcast_to(taps[kind : kind + 1], (plan.cols, width))
                spread = pltpu.roll(spread, 0, 1, stride=1, stride_axis=0)
                out[index, kind * plan.cols : (kind + 1) * plan.cols] = spread.astype(jnp.bfloat16)
            index += 1


def make_taps(plan, support):
    kinds, entries = support.shape[2:]
    count = sum(len(plan.sources(slot)) for slot in range(plan.rows))
    width = -(-plan.lon_total // lanes) * lanes
    return pl.pallas_call(
        functools.partial(taps_body, plan, kinds, entries),
        out_shape=jax.ShapeDtypeStruct((count, kinds * plan.cols, width), jnp.bfloat16),
        in_specs=[vmem],
        out_specs=vmem,
        name="filter_taps",
    )(support)


def compute_body(plan, kinds, *refs):
    x_ref, low_ref, high_ref = refs[:3]
    used = 3 + len(plan.moves)
    got_refs = refs[3:used]
    taps_ref, mix_ref, gain_ref, up_ref, down_ref, out_ref, win, response = refs[used:]
    rows, cols = plan.rows, plan.cols
    south = is_south(plan)
    middle = (plan.half - 1) * cols
    for slot in range(0 if plan.outer else 1, rows + 2):
        win[slot, middle : middle + cols] = load_slot(plan, south, slot, x_ref, low_ref, high_ref)
    for (dist, sign, picks, _), got in zip(plan.moves, got_refs):
        place = middle + sign * dist * cols
        for slot, start, width in picks:
            block = got[start : start + width]
            if width < cols:
                gap = jnp.zeros((cols - width, block.shape[1]), block.dtype)
                block = jnp.concatenate([block, gap] if sign == 1 else [gap, block], axis=0)
            win[slot, place : place + cols] = block
    index = 0
    for slot in range(rows):
        first, count = plan.span(slot)
        total = None
        for source in plan.sources(slot):
            piece = jnp.dot(
                taps_ref[index, :, :count],
                win[source, first : first + count],
                preferred_element_type=jnp.float32,
            )
            total = piece if total is None else total + piece
            index += 1
        total = total.astype(jnp.bfloat16)
        for kind in range(kinds):
            response[kind, slot * cols : (slot + 1) * cols] = total[kind * cols : (kind + 1) * cols]
    mixed = jnp.dot(response[0], mix_ref[0], preferred_element_type=jnp.float32)
    for kind in range(1, kinds):
        mixed = mixed + jnp.dot(response[kind], mix_ref[kind], preferred_element_type=jnp.float32)
    own = win[1 : rows + 1, middle : middle + cols].reshape(rows * cols, -1)
    latent = own.astype(jnp.float32) + mixed
    mean = jnp.mean(latent, axis=1, keepdims=True)
    variance = jnp.mean(jnp.square(latent - mean), axis=1, keepdims=True)
    normed = (latent - mean) * lax.rsqrt(variance + norm_eps) * gain_ref[...]
    hidden = jnp.dot(normed.astype(jnp.bfloat16), up_ref[...], preferred_element_type=jnp.float32)
    hidden = (0.5 * hidden * (1.0 + lax.erf(hidden * 0.5**0.5))).astype(jnp.bfloat16)
    output = latent + jnp.dot(hidden, down_ref[...], preferred_element_type=jnp.float32)
    output = output.astype(jnp.bfloat16)
    for slot in range(rows):
        out_ref[row_of(plan, south, slot + 1)] = output[slot * cols : (slot + 1) * cols]


def on_device(
    fields,
    support_rows,
    support_lons,
    support_weights,
    mix_weight,
    norm_gain,
    up_weight,
    down_weight,
):
    channels, rows, cols = fields.shape
    kinds = support_rows.shape[0]
    lon_shards = lax.axis_size("lon")
    lat_shards = lax.axis_size("lat")
    plan = Plan(rows, cols, lat_shards, lon_shards)
    x = jnp.transpose(fields, (1, 2, 0))
    forward = [(i, i + 1) for i in range(lat_shards - 1)]
    low = lax.ppermute(x[rows - 1 :], "lat", forward)
    high = lax.ppermute(x[:1], "lat", [(b, a) for a, b in forward])

    edge = (0, rows + 1)
    inside = [m for m in plan.moves if all(slot not in edge for slot, _, _ in m[2])]
    across = [m for m in plan.moves if m not in inside]
    sent = {}
    if inside:
        sent.update(zip([m[:2] for m in inside], pack(plan, inside, x, None, None)))
    sent.update(zip([m[:2] for m in across], pack(plan, across, x, low, high)))
    got = [
        lax.ppermute(
            sent[dist, sign],
            "lon",
            [((i + sign * dist) % lon_shards, i) for i in range(lon_shards)],
        )
        for dist, sign, _, _ in plan.moves
    ]
    support = jnp.stack(
        [
            support_rows.astype(jnp.float32),
            support_lons.astype(jnp.float32),
            support_weights,
        ]
    ).transpose(2, 0, 1, 3)
    taps = make_taps(plan, support)
    args = (x, low, high, *got, taps, mix_weight, norm_gain[None], up_weight, down_weight)
    output = pl.pallas_call(
        functools.partial(compute_body, plan, kinds),
        out_shape=jax.ShapeDtypeStruct((rows, cols, channels), jnp.bfloat16),
        in_specs=[vmem] * len(args),
        out_specs=vmem,
        scratch_shapes=[
            pltpu.VMEM((rows + 2, plan.lon_total, channels), jnp.bfloat16),
            pltpu.VMEM((kinds, rows * cols, channels), jnp.bfloat16),
        ],
        compiler_params=pltpu.CompilerParams(vmem_limit_bytes=40 * 2**20),
        name="filter_mix_mlp",
    )(*args)
    return jnp.transpose(output, (2, 0, 1))


def solution(mesh):
    in_specs = (P("member", "lat", "lon"), P(), P(), P(), P(), P(), P(), P())
    out_specs = P("member", "lat", "lon")
    return jax.shard_map(
        on_device, mesh=mesh, in_specs=in_specs, out_specs=out_specs, check_vma=False
    )
```

```python
import functools

import jax
import jax.numpy as jnp
from jax import lax
from jax.experimental import pallas as pl
from jax.experimental.pallas import tpu as pltpu
from jax.sharding import PartitionSpec as P

norm_eps = 1e-05
lanes = 128
mib = 2**20
vmem = pl.BlockSpec(memory_space=pltpu.VMEM)
anywhere = pl.BlockSpec(memory_space=pl.ANY)


class Plan:
    def __init__(self, rows, cols, lat_shards, lon_shards):
        self.rows, self.cols = rows, cols
        self.lat_shards, self.lon_shards = lat_shards, lon_shards
        lat_total, lon_total = rows * lat_shards, cols * lon_shards
        self.lon_total = lon_total
        self.half = half = lon_shards // 2
        self.outer = lat_shards > 2
        reach = [0] * rows
        need = [0] * (rows + 2)
        for shard in range(lat_shards // 2):
            for slot in range(rows):
                row = shard * rows + slot
                span = min(lon_total // 2, 4 * lat_total // min(row + 1, lat_total - row))
                reach[slot] = max(reach[slot], span)
                for source in (slot, slot + 1, slot + 2):
                    if shard > 0 or source > 0:
                        need[source] = max(need[source], span)
        self.blocks = [min(half, -(-span // cols)) for span in reach]
        self.moves = {}
        for dist in range(1, half + 1):
            for sign in (1, -1):
                picks, start = [], 0
                for slot in range(1, rows + 1):
                    if dist >= half - 1:
                        width = cols if need[slot] > (half - 2) * cols else 0
                    else:
                        width = max(0, min(cols, need[slot] - (dist - 1) * cols))
                    if width > 0:
                        picks.append((slot, start, width))
                        start += width
                if picks and (dist < half or sign == 1):
                    self.moves[dist, sign] = picks
        self.margin = max(need[0], need[rows + 1])
        self.margin_blocks = -(-self.margin // cols)

    def payload(self, move):
        _, start, width = self.moves[move][-1]
        return start + width

    def span(self, slot):
        blocks = self.blocks[slot]
        if blocks == self.half:
            return 0, self.lon_total
        return (self.half - 1 - blocks) * self.cols, (2 * blocks + 1) * self.cols

    def sources(self, slot):
        return [s for s in (slot, slot + 1, slot + 2) if s > 0 or self.outer]


def is_south(plan):
    return lax.axis_index("lat") >= plan.lat_shards // 2


def row_of(plan, south, slot):
    return jnp.where(south, plan.rows - slot, slot - 1)


def pack_body(plan, moves, x_ref, *outs):
    south = is_south(plan)
    for move, out in zip(moves, outs):
        for slot, start, width in plan.moves[move]:
            block = x_ref[row_of(plan, south, slot)]
            block = block[:width] if move[1] == 1 else block[plan.cols - width :]
            out[start : start + width] = block


def pack(plan, moves, x):
    return pl.pallas_call(
        functools.partial(pack_body, plan, moves),
        out_shape=[jax.ShapeDtypeStruct((plan.payload(m), x.shape[2]), x.dtype) for m in moves],
        in_specs=[vmem],
        out_specs=[vmem] * len(moves),
        compiler_params=pltpu.CompilerParams(vmem_limit_bytes=8 * mib),
        name="pack_columns",
    )(x)


def strip_of(plan, slot, south, x_ref, got):
    parts = [x_ref[row_of(plan, south, slot)]]
    for dist in range(1, plan.margin_blocks + 1):
        width = min(plan.cols, plan.margin - (dist - 1) * plan.cols)
        for sign in (1, -1):
            (pick,) = [p for p in plan.moves[dist, sign] if p[0] == slot]
            _, start, held = pick
            if sign == 1:
                parts.append(got[dist, sign][start : start + width])
            else:
                parts.insert(0, got[dist, sign][start + held - width : start + held])
    return jnp.concatenate(parts, axis=0)


def strip_body(plan, moves, x_ref, *refs):
    got = dict(zip(moves, refs))
    outs = refs[len(moves) :]
    south = is_south(plan)
    inner = strip_of(plan, plan.rows, south, x_ref, got)
    if not plan.outer:
        outs[0][...] = inner
        return
    outer = strip_of(plan, 1, south, x_ref, got)
    outs[0][...] = jnp.where(south, outer, inner)
    outs[1][...] = jnp.where(south, inner, outer)


def edge_rows(plan, x, got):
    moves = [m for m in plan.moves if m[0] <= plan.margin_blocks]
    count = 2 if plan.outer else 1
    size = plan.cols + 2 * plan.margin
    strips = pl.pallas_call(
        functools.partial(strip_body, plan, moves),
        out_shape=[jax.ShapeDtypeStruct((size, x.shape[2]), x.dtype)] * count,
        in_specs=[vmem] * (1 + len(moves)),
        out_specs=[vmem] * count,
        compiler_params=pltpu.CompilerParams(vmem_limit_bytes=8 * mib),
        name="pack_edge_row",
    )(x, *[got[m] for m in moves])
    if not plan.outer:
        return [lax.ppermute(strips[0], "lat", [(0, 1), (1, 0)])]
    forward = [(i, i + 1) for i in range(plan.lat_shards - 1)]
    low = lax.ppermute(strips[0], "lat", forward)
    high = lax.ppermute(strips[1], "lat", [(b, a) for a, b in forward])
    return [low, high]


def taps_body(plan, entries, lift_ref, place_ref, weight_ref, out):
    size, lat_total = lift_ref.shape
    cols, width = plan.cols, out.shape[2]
    south = is_south(plan)
    row_start = lax.axis_index("lat") * plan.rows
    source_row = lax.broadcasted_iota(jnp.int32, (lat_total, width), 0)
    spot = lax.broadcasted_iota(jnp.int32, (size, width), 1)
    early = lax.broadcasted_iota(jnp.int32, (size, width), 0) // entries * cols
    kinds_rows = size // entries * cols
    basis_row = lax.broadcasted_iota(jnp.int32, (kinds_rows, size), 0) // cols
    basis_col = lax.broadcasted_iota(jnp.int32, (kinds_rows, size), 1) // entries
    gather = jnp.where(basis_row == basis_col, 1.0, 0.0).astype(jnp.bfloat16)
    tables = [ref[...].astype(jnp.bfloat16) for ref in (lift_ref, place_ref, weight_ref)]
    index = 0
    for slot in range(plan.rows):
        center = (plan.half - 1) * cols - plan.span(slot)[0]
        here = source_row == row_start + row_of(plan, south, slot + 1)
        here = jnp.where(here, 1.0, 0.0).astype(jnp.bfloat16)
        lift, place, weight = [
            jnp.dot(table, here, preferred_element_type=jnp.float32) for table in tables
        ]
        lift = jnp.where(south, -lift, lift)
        want = spot + early - center
        gap = want - place.astype(jnp.int32)
        hit = lax.rem(gap + 4 * width, width) == 0
        weight = jnp.where(hit, weight, 0.0)
        for source in plan.sources(slot):
            part = jnp.where(lift == float(source - slot - 1), weight, 0.0).astype(jnp.bfloat16)
            taps = jnp.dot(gather, part, preferred_element_type=jnp.float32)
            taps = pltpu.roll(taps, 0, 1, stride=1, stride_axis=0)
            out[index] = taps.astype(jnp.bfloat16)
            index += 1


def make_taps(plan, support):
    kinds, _, entries = support[0].shape
    count = sum(len(plan.sources(slot)) for slot in range(plan.rows))
    width = -(-plan.lon_total // lanes) * lanes
    tables = [s.transpose(0, 2, 1).reshape(kinds * entries, -1) for s in support]
    return pl.pallas_call(
        functools.partial(taps_body, plan, entries),
        out_shape=jax.ShapeDtypeStruct((count, kinds * plan.cols, width), jnp.bfloat16),
        in_specs=[vmem] * 3,
        out_specs=vmem,
        compiler_params=pltpu.CompilerParams(vmem_limit_bytes=8 * mib),
        cost_estimate=pl.CostEstimate(flops=3 * 10**9, bytes_accessed=10**7, transcendentals=0),
        name="filter_taps",
    )(*tables)


def fill_window(plan, sources, south, x_ref, got, edges, win):
    rows, cols = plan.rows, plan.cols
    middle = (plan.half - 1) * cols
    for slot in sources:
        if slot in (0, rows + 1):
            strip = edges[0][...]
            if plan.outer:
                first, last = (edges[1], edges[0]) if slot == 0 else (edges[0], edges[1])
                strip = jnp.where(south, first[...], last[...])
            gap = plan.margin_blocks * cols - plan.margin
            if gap > 0:
                gap = jnp.zeros((gap, strip.shape[1]), strip.dtype)
                strip = jnp.concatenate([gap, strip, gap], axis=0)
            start = middle - plan.margin_blocks * cols
            win[slot - sources[0], start : start + strip.shape[0]] = strip
        else:
            win[slot - sources[0], middle : middle + cols] = x_ref[row_of(plan, south, slot)]
    for (dist, sign), ref in got.items():
        place = middle + sign * dist * cols
        for slot, start, width in plan.moves[dist, sign]:
            if slot not in sources:
                continue
            block = ref[start : start + width]
            if width < cols:
                gap = jnp.zeros((cols - width, block.shape[1]), block.dtype)
                block = jnp.concatenate([block, gap] if sign == 1 else [gap, block], axis=0)
            win[slot - sources[0], place : place + cols] = block


def compute_body(plan, slots, moves, edge_count, chained, *refs):
    x_ref = refs[0]
    got = dict(zip(moves, refs[1:]))
    used = 1 + len(moves)
    edges = refs[used : used + edge_count]
    used += edge_count
    taps_ref, mix_ref, gain_ref, up_ref, down_ref = refs[used : used + 5]
    used += 5 + chained
    out_ref, win, response, result, sem = refs[used:]
    rows, cols = plan.rows, plan.cols
    kinds = mix_ref.shape[0]
    south = is_south(plan)
    middle = (plan.half - 1) * cols
    sources = sorted({s for slot in slots for s in plan.sources(slot)})
    fill_window(plan, sources, south, x_ref, got, edges, win)
    for order, slot in enumerate(slots):
        first, count = plan.span(slot)
        index = sum(len(plan.sources(s)) for s in range(slot))
        total = None
        for source in plan.sources(slot):
            piece = jnp.dot(
                taps_ref[index, :, :count],
                win[source - sources[0], first : first + count],
                preferred_element_type=jnp.float32,
            )
            total = piece if total is None else total + piece
            index += 1
        total = total.astype(jnp.bfloat16)
        for kind in range(kinds):
            place = slice(order * cols, (order + 1) * cols)
            response[kind, place] = total[kind * cols : (kind + 1) * cols]
    mixed = jnp.dot(response[0], mix_ref[0], preferred_element_type=jnp.float32)
    for kind in range(1, kinds):
        mixed = mixed + jnp.dot(response[kind], mix_ref[kind], preferred_element_type=jnp.float32)
    start = slots[0] + 1 - sources[0]
    own = win[start : start + len(slots), middle : middle + cols]
    latent = own.reshape(len(slots) * cols, -1).astype(jnp.float32) + mixed
    mean = jnp.mean(latent, axis=1, keepdims=True)
    variance = jnp.mean(jnp.square(latent - mean), axis=1, keepdims=True)
    normed = (latent - mean) * lax.rsqrt(variance + norm_eps) * gain_ref[...]
    hidden = jnp.dot(normed.astype(jnp.bfloat16), up_ref[...], preferred_element_type=jnp.float32)
    hidden = (0.5 * hidden * (1.0 + lax.erf(hidden * 0.5**0.5))).astype(jnp.bfloat16)
    output = latent + jnp.dot(hidden, down_ref[...], preferred_element_type=jnp.float32)
    output = output.astype(jnp.bfloat16)
    for order in range(len(slots)):
        spot = jnp.where(south, len(slots) - 1 - order, order)
        result[spot] = output[order * cols : (order + 1) * cols]
    first_row = jnp.where(south, rows - 1 - slots[-1], slots[0])
    copy = pltpu.make_async_copy(result, out_ref.at[pl.ds(first_row, len(slots))], sem)
    copy.start()
    copy.wait()


def compute(plan, slots, x, got, edges, taps, weights, chain):
    sources = sorted({s for slot in slots for s in plan.sources(slot)})
    moves = [m for m, picks in plan.moves.items() if any(p[0] in sources for p in picks)]
    reach = max(plan.blocks[slot] for slot in slots)
    moves = [m for m in moves if m[0] <= reach]
    edges = edges if set(sources) & {0, plan.rows + 1} else []
    args = [x, *[got[m] for m in moves], *edges, taps, *weights]
    specs = [vmem] * len(args)
    if chain is not None:
        args.append(chain)
        specs.append(anywhere)
    channels = x.shape[2]
    kinds = weights[0].shape[0]
    return pl.pallas_call(
        functools.partial(compute_body, plan, slots, moves, len(edges), chain is not None),
        out_shape=jax.ShapeDtypeStruct(x.shape, x.dtype),
        in_specs=specs,
        out_specs=anywhere,
        scratch_shapes=[
            pltpu.VMEM((len(sources), plan.lon_total, channels), x.dtype),
            pltpu.VMEM((kinds, len(slots) * plan.cols, channels), x.dtype),
            pltpu.VMEM((len(slots), plan.cols, channels), x.dtype),
            pltpu.SemaphoreType.DMA,
        ],
        input_output_aliases={} if chain is None else {len(args) - 1: 0},
        compiler_params=pltpu.CompilerParams(vmem_limit_bytes=24 * mib),
        cost_estimate=pl.CostEstimate(flops=10**6, bytes_accessed=10**5, transcendentals=0),
        name="filter_mix_mlp",
    )(*args)


def on_device(
    fields,
    support_rows,
    support_lons,
    support_weights,
    mix_weight,
    norm_gain,
    up_weight,
    down_weight,
):
    channels, rows, cols = fields.shape
    count = lax.axis_size("lon")
    plan = Plan(rows, cols, lax.axis_size("lat"), count)
    half = plan.half
    x = jnp.transpose(fields, (1, 2, 0))

    direct = [m for m in plan.moves if m[0] < half - 1 or m[0] == half]
    sent = dict(zip(direct, pack(plan, direct, x)))

    def shifted(value, step):
        return lax.ppermute(value, "lon", [((i + step) % count, i) for i in range(count)])

    got = {m: shifted(sent[m], m[0] * m[1]) for m in direct}
    taps = make_taps(plan, (support_rows, support_lons, support_weights))
    first = [m for m in got if m[0] <= plan.margin_blocks or m[0] == half]
    joined, taps = lax.optimization_barrier(([got[m] for m in first], taps))
    got.update(zip(first, joined))
    if (half - 1, 1) in plan.moves and half > 2:
        got[half - 1, 1] = shifted(got[half, 1], -1)
        got[half - 1, -1] = shifted(got[half, 1], 1)
    edges = edge_rows(plan, x, got)
    weights = (mix_weight, norm_gain[None], up_weight, down_weight)
    near = [slot for slot in range(rows) if plan.blocks[slot] <= 1]
    far = [slot for slot in range(rows) if plan.blocks[slot] > 1]
    output = None
    for slots in (near, far):
        if slots:
            output = compute(plan, slots, x, got, edges, taps, weights, output)
    return jnp.transpose(output, (2, 0, 1))


def solution(mesh):
    in_specs = (P("member", "lat", "lon"), P(), P(), P(), P(), P(), P(), P())
    out_specs = P("member", "lat", "lon")
    return jax.shard_map(
        on_device, mesh=mesh, in_specs=in_specs, out_specs=out_specs, check_vma=False
    )
```

```python
import functools

import jax
import jax.numpy as jnp
from jax import lax
from jax.experimental import pallas as pl
from jax.experimental.pallas import tpu as pltpu
from jax.sharding import PartitionSpec as P

norm_eps = 1e-05
lanes = 128
mib = 2**20
vmem = pl.BlockSpec(memory_space=pltpu.VMEM)
anywhere = pl.BlockSpec(memory_space=pl.ANY)


class Plan:
    def __init__(self, rows, cols, lat_shards, lon_shards):
        self.rows, self.cols = rows, cols
        self.lat_shards, self.lon_shards = lat_shards, lon_shards
        lat_total, lon_total = rows * lat_shards, cols * lon_shards
        self.lon_total = lon_total
        self.half = half = lon_shards // 2
        self.outer = lat_shards > 2
        reach = [0] * rows
        need = [0] * (rows + 2)
        for shard in range(lat_shards // 2):
            for slot in range(rows):
                row = shard * rows + slot
                span = min(lon_total // 2, 4 * lat_total // min(row + 1, lat_total - row))
                reach[slot] = max(reach[slot], span)
                for source in (slot, slot + 1, slot + 2):
                    if shard > 0 or source > 0:
                        need[source] = max(need[source], span)
        self.blocks = [min(half, -(-span // cols)) for span in reach]
        self.moves = {}
        for dist in range(1, half + 1):
            for sign in (1, -1):
                picks, start = [], 0
                for slot in range(1, rows + 1):
                    if dist >= half - 1:
                        width = cols if need[slot] > (half - 2) * cols else 0
                    else:
                        width = max(0, min(cols, need[slot] - (dist - 1) * cols))
                    if width > 0:
                        picks.append((slot, start, width))
                        start += width
                if picks and (dist < half or sign == 1):
                    self.moves[dist, sign] = picks
        self.margin = max(need[0], need[rows + 1])
        self.margin_blocks = -(-self.margin // cols)

    def payload(self, move):
        _, start, width = self.moves[move][-1]
        return start + width

    def span(self, slot):
        blocks = self.blocks[slot]
        if blocks == self.half:
            return 0, self.lon_total
        return (self.half - 1 - blocks) * self.cols, (2 * blocks + 1) * self.cols

    def taps_width(self, slot):
        return -(-len(self.sources(slot)) * self.span(slot)[1] // lanes) * lanes

    def sources(self, slot):
        return [s for s in (slot, slot + 1, slot + 2) if s > 0 or self.outer]


def is_south(plan):
    return lax.axis_index("lat") >= plan.lat_shards // 2


def row_of(plan, south, slot):
    return jnp.where(south, plan.rows - slot, slot - 1)


def pack_body(plan, moves, x_ref, *outs):
    south = is_south(plan)
    for move, out in zip(moves, outs):
        for slot, start, width in plan.moves[move]:
            block = x_ref[row_of(plan, south, slot)]
            block = block[:width] if move[1] == 1 else block[plan.cols - width :]
            out[start : start + width] = block


def pack(plan, moves, x):
    return pl.pallas_call(
        functools.partial(pack_body, plan, moves),
        out_shape=[jax.ShapeDtypeStruct((plan.payload(m), x.shape[2]), x.dtype) for m in moves],
        in_specs=[vmem],
        out_specs=[vmem] * len(moves),
        compiler_params=pltpu.CompilerParams(vmem_limit_bytes=8 * mib),
        name="pack_columns",
    )(x)


def strip_of(plan, slot, south, x_ref, got):
    parts = [x_ref[row_of(plan, south, slot)]]
    for dist in range(1, plan.margin_blocks + 1):
        width = min(plan.cols, plan.margin - (dist - 1) * plan.cols)
        for sign in (1, -1):
            (pick,) = [p for p in plan.moves[dist, sign] if p[0] == slot]
            _, start, held = pick
            if sign == 1:
                parts.append(got[dist, sign][start : start + width])
            else:
                parts.insert(0, got[dist, sign][start + held - width : start + held])
    return jnp.concatenate(parts, axis=0)


def strip_body(plan, moves, x_ref, *refs):
    got = dict(zip(moves, refs))
    outs = refs[len(moves) :]
    south = is_south(plan)
    inner = strip_of(plan, plan.rows, south, x_ref, got)
    if not plan.outer:
        outs[0][...] = inner
        return
    outer = strip_of(plan, 1, south, x_ref, got)
    outs[0][...] = jnp.where(south, outer, inner)
    outs[1][...] = jnp.where(south, inner, outer)


def edge_rows(plan, x, got):
    moves = [m for m in plan.moves if m[0] <= plan.margin_blocks]
    count = 2 if plan.outer else 1
    size = plan.cols + 2 * plan.margin
    strips = pl.pallas_call(
        functools.partial(strip_body, plan, moves),
        out_shape=[jax.ShapeDtypeStruct((size, x.shape[2]), x.dtype)] * count,
        in_specs=[vmem] * (1 + len(moves)),
        out_specs=[vmem] * count,
        compiler_params=pltpu.CompilerParams(vmem_limit_bytes=8 * mib),
        name="pack_edge_row",
    )(x, *[got[m] for m in moves])
    if not plan.outer:
        return [lax.ppermute(strips[0], "lat", [(0, 1), (1, 0)])]
    forward = [(i, i + 1) for i in range(plan.lat_shards - 1)]
    low = lax.ppermute(strips[0], "lat", forward)
    high = lax.ppermute(strips[1], "lat", [(b, a) for a, b in forward])
    return [low, high]


def taps_body(plan, entries, lift_ref, place_ref, weight_ref, out):
    size, lat_total = lift_ref.shape
    cols, width = plan.cols, out.shape[2]
    south = is_south(plan)
    row_start = lax.axis_index("lat") * plan.rows
    source_row = lax.broadcasted_iota(jnp.int32, (lat_total, lanes), 0)
    spot = lax.broadcasted_iota(jnp.int32, (size, width), 1)
    early = lax.broadcasted_iota(jnp.int32, (size, width), 0) // entries * cols
    kinds_rows = size // entries * cols
    basis_row = lax.broadcasted_iota(jnp.int32, (kinds_rows, size), 0) // cols
    basis_col = lax.broadcasted_iota(jnp.int32, (kinds_rows, size), 1) // entries
    gather = jnp.where(basis_row == basis_col, 1.0, 0.0).astype(jnp.bfloat16)
    tables = [ref[...].astype(jnp.bfloat16) for ref in (lift_ref, place_ref, weight_ref)]
    for slot in range(plan.rows):
        first, count = plan.span(slot)
        center = (plan.half - 1) * cols - first
        here = source_row == row_start + row_of(plan, south, slot + 1)
        here = jnp.where(here, 1.0, 0.0).astype(jnp.bfloat16)
        lift, place, weight = [
            jnp.dot(table, here, preferred_element_type=jnp.float32) for table in tables
        ]
        lift = jnp.where(south, -lift, lift).astype(jnp.int32)
        place = place.astype(jnp.int32) + center
        sources = plan.sources(slot)
        if count == plan.lon_total:
            pieces = [(source - slot - 1, order * count) for order, source in enumerate(sources)]
            size = count
        else:
            place = place + (lift + slot + 1 - sources[0]) * count
            pieces, size = [(None, 0)], plan.taps_width(slot)
        for offset, start in pieces:
            gap = spot[:, :size] + early[:, :size] - place[:, :1]
            hit = lax.rem(gap + 4 * size, size) == 0
            if offset is not None:
                hit = hit & (lift[:, :1] == offset)
            part = jnp.where(hit, weight[:, :1], 0.0).astype(jnp.bfloat16)
            taps = jnp.dot(gather, part, preferred_element_type=jnp.float32)
            taps = pltpu.roll(taps, 0, 1, stride=1, stride_axis=0)
            out[slot, :, start : start + size] = taps.astype(jnp.bfloat16)


def make_taps(plan, support):
    kinds, _, entries = support[0].shape
    width = max(plan.taps_width(slot) for slot in range(plan.rows))
    tables = [s.transpose(0, 2, 1).reshape(kinds * entries, -1) for s in support]
    return pl.pallas_call(
        functools.partial(taps_body, plan, entries),
        out_shape=jax.ShapeDtypeStruct((plan.rows, kinds * plan.cols, width), jnp.bfloat16),
        in_specs=[vmem] * 3,
        out_specs=vmem,
        compiler_params=pltpu.CompilerParams(vmem_limit_bytes=8 * mib),
        cost_estimate=pl.CostEstimate(flops=3 * 10**9, bytes_accessed=10**7, transcendentals=0),
        name="filter_taps",
    )(*tables)


def fill_window(plan, sources, south, x_ref, got, edges, win):
    rows, cols = plan.rows, plan.cols
    middle = (plan.half - 1) * cols
    for slot in sources:
        if slot in (0, rows + 1):
            strip = edges[0][...]
            if plan.outer:
                first, last = (edges[1], edges[0]) if slot == 0 else (edges[0], edges[1])
                strip = jnp.where(south, first[...], last[...])
            gap = plan.margin_blocks * cols - plan.margin
            if gap > 0:
                gap = jnp.zeros((gap, strip.shape[1]), strip.dtype)
                strip = jnp.concatenate([gap, strip, gap], axis=0)
            start = middle - plan.margin_blocks * cols
            win[sources.index(slot), start : start + strip.shape[0]] = strip
        else:
            win[sources.index(slot), middle : middle + cols] = x_ref[row_of(plan, south, slot)]
    for (dist, sign), ref in got.items():
        place = middle + sign * dist * cols
        for slot, start, width in plan.moves[dist, sign]:
            if slot not in sources:
                continue
            block = ref[start : start + width]
            if width < cols:
                gap = jnp.zeros((cols - width, block.shape[1]), block.dtype)
                block = jnp.concatenate([block, gap] if sign == 1 else [gap, block], axis=0)
            win[sources.index(slot), place : place + cols] = block


def compute_body(plan, slots, moves, edge_count, chained, *refs):
    x_ref = refs[0]
    got = dict(zip(moves, refs[1:]))
    used = 1 + len(moves)
    edges = refs[used : used + edge_count]
    used += edge_count
    taps_ref, mix_ref, gain_ref, up_ref, down_ref = refs[used : used + 5]
    used += 5 + chained
    out_ref, win, response, result, sem = refs[used:]
    rows, cols = plan.rows, plan.cols
    kinds = mix_ref.shape[0]
    south = is_south(plan)
    middle = (plan.half - 1) * cols
    sources = sorted({s for slot in slots for s in plan.sources(slot)})
    fill_window(plan, sources, south, x_ref, got, edges, win)
    for order, slot in enumerate(slots):
        first, count = plan.span(slot)
        found = [win[sources.index(s), first : first + count] for s in plan.sources(slot)]
        total = jnp.dot(
            taps_ref[slot, :, : count * len(found)],
            jnp.concatenate(found, axis=0),
            preferred_element_type=jnp.float32,
        )
        total = total.astype(jnp.bfloat16)
        for kind in range(kinds):
            place = slice(order * cols, (order + 1) * cols)
            response[kind, place] = total[kind * cols : (kind + 1) * cols]
    mixed = jnp.dot(response[0], mix_ref[0], preferred_element_type=jnp.float32)
    for kind in range(1, kinds):
        mixed = mixed + jnp.dot(response[kind], mix_ref[kind], preferred_element_type=jnp.float32)
    own = [win[sources.index(slot + 1), middle : middle + cols] for slot in slots]
    latent = jnp.concatenate(own, axis=0).astype(jnp.float32) + mixed
    mean = jnp.mean(latent, axis=1, keepdims=True)
    variance = jnp.mean(jnp.square(latent - mean), axis=1, keepdims=True)
    normed = (latent - mean) * lax.rsqrt(variance + norm_eps) * gain_ref[...]
    hidden = jnp.dot(normed.astype(jnp.bfloat16), up_ref[...], preferred_element_type=jnp.float32)
    hidden = (0.5 * hidden * (1.0 + lax.erf(hidden * 0.5**0.5))).astype(jnp.bfloat16)
    output = latent + jnp.dot(hidden, down_ref[...], preferred_element_type=jnp.float32)
    output = output.astype(jnp.bfloat16)
    copies = []
    for number, (offset, run) in enumerate(runs_of(slots)):
        size = len(run)
        for order in range(size):
            spot = offset + jnp.where(south, size - 1 - order, order)
            place = (offset + order) * cols
            result[spot] = output[place : place + cols]
        first_row = jnp.where(south, rows - 1 - run[-1], run[0])
        source = result.at[pl.ds(offset, size)]
        target = out_ref.at[pl.ds(first_row, size)]
        copies.append(pltpu.make_async_copy(source, target, sem.at[number]))
        copies[-1].start()
    for copy in copies:
        copy.wait()


def runs_of(slots):
    runs = []
    for position, slot in enumerate(slots):
        if runs and runs[-1][1][-1] + 1 == slot:
            runs[-1][1].append(slot)
        else:
            runs.append((position, [slot]))
    return runs


def compute(plan, slots, x, got, edges, taps, weights, chain):
    sources = sorted({s for slot in slots for s in plan.sources(slot)})
    moves = [m for m, picks in plan.moves.items() if any(p[0] in sources for p in picks)]
    reach = max(plan.blocks[slot] for slot in slots)
    moves = [m for m in moves if m[0] <= reach]
    edges = edges if set(sources) & {0, plan.rows + 1} else []
    args = [x, *[got[m] for m in moves], *edges, taps, *weights]
    specs = [vmem] * len(args)
    if chain is not None:
        args.append(chain)
        specs.append(anywhere)
    channels = x.shape[2]
    kinds = weights[0].shape[0]
    return pl.pallas_call(
        functools.partial(compute_body, plan, slots, moves, len(edges), chain is not None),
        out_shape=jax.ShapeDtypeStruct(x.shape, x.dtype),
        in_specs=specs,
        out_specs=anywhere,
        scratch_shapes=[
            pltpu.VMEM((len(sources), plan.lon_total, channels), x.dtype),
            pltpu.VMEM((kinds, len(slots) * plan.cols, channels), x.dtype),
            pltpu.VMEM((len(slots), plan.cols, channels), x.dtype),
            pltpu.SemaphoreType.DMA((len(runs_of(slots)),)),
        ],
        input_output_aliases={} if chain is None else {len(args) - 1: 0},
        compiler_params=pltpu.CompilerParams(vmem_limit_bytes=24 * mib),
        cost_estimate=pl.CostEstimate(flops=10**6, bytes_accessed=10**5, transcendentals=0),
        name="filter_mix_mlp",
    )(*args)


def on_device(
    fields,
    support_rows,
    support_lons,
    support_weights,
    mix_weight,
    norm_gain,
    up_weight,
    down_weight,
):
    channels, rows, cols = fields.shape
    count = lax.axis_size("lon")
    plan = Plan(rows, cols, lax.axis_size("lat"), count)
    half = plan.half
    x = jnp.transpose(fields, (1, 2, 0))

    direct = [m for m in plan.moves if m[0] < half - 1 or m[0] == half]
    close = [m for m in direct if m[0] == 1]
    wide = [m for m in direct if m[0] > 1]
    sent = dict(zip(close, pack(plan, close, x)))
    later, sent[1, 1], sent[1, -1] = lax.optimization_barrier((x, sent[1, 1], sent[1, -1]))
    sent.update(zip(wide, pack(plan, wide, later)))

    def shifted(value, step):
        return lax.ppermute(value, "lon", [((i + step) % count, i) for i in range(count)])

    got = {m: shifted(sent[m], m[0] * m[1]) for m in direct}
    forward = (half - 1, 1) in plan.moves and half > 2
    if forward:
        got[half - 1, 1] = shifted(got[half, 1], -1)
    taps = make_taps(plan, (support_rows, support_lons, support_weights))
    if forward:
        opposite, taps = lax.optimization_barrier((got[half, 1], taps))
        got[half - 1, -1] = shifted(opposite, 1)
    first = [m for m in got if m[0] <= plan.margin_blocks]
    joined, taps = lax.optimization_barrier(([got[m] for m in first], taps))
    got.update(zip(first, joined))
    edges = edge_rows(plan, x, got)
    weights = (mix_weight, norm_gain[None], up_weight, down_weight)
    inner = range(1 if plan.outer else 0, rows - 1)
    near = [slot for slot in inner if plan.blocks[slot] <= 1]
    far = [slot for slot in range(rows) if slot not in near]
    output = None
    for slots in (near, far):
        if slots:
            output = compute(plan, slots, x, got, edges, taps, weights, output)
    return jnp.transpose(output, (2, 0, 1))


def solution(mesh):
    in_specs = (P("member", "lat", "lon"), P(), P(), P(), P(), P(), P(), P())
    out_specs = P("member", "lat", "lon")
    return jax.shard_map(
        on_device, mesh=mesh, in_specs=in_specs, out_specs=out_specs, check_vma=False
    )
```

```python
import functools

import jax
import jax.numpy as jnp
from jax import lax
from jax.experimental import pallas as pl
from jax.experimental.pallas import tpu as pltpu
from jax.sharding import PartitionSpec as P

norm_eps = 1e-05
lanes = 128
mib = 2**20
vmem = pl.BlockSpec(memory_space=pltpu.VMEM)
anywhere = pl.BlockSpec(memory_space=pl.ANY)


class Plan:
    def __init__(self, rows, cols, lat_shards, lon_shards):
        self.rows, self.cols = rows, cols
        self.lat_shards, self.lon_shards = lat_shards, lon_shards
        lat_total, lon_total = rows * lat_shards, cols * lon_shards
        self.lon_total = lon_total
        self.half = half = lon_shards // 2
        self.outer = lat_shards > 2
        reach = [0] * rows
        need = [0] * (rows + 2)
        for shard in range(lat_shards // 2):
            for slot in range(rows):
                row = shard * rows + slot
                span = min(lon_total // 2, 4 * lat_total // min(row + 1, lat_total - row))
                reach[slot] = max(reach[slot], span)
                for source in (slot, slot + 1, slot + 2):
                    if shard > 0 or source > 0:
                        need[source] = max(need[source], span)
        self.blocks = [min(half, -(-span // cols)) for span in reach]
        self.moves = {}
        for dist in range(1, half + 1):
            for sign in (1, -1):
                picks, start = [], 0
                for slot in range(1, rows + 1):
                    if dist >= half - 1:
                        width = cols if need[slot] > (half - 2) * cols else 0
                    else:
                        width = max(0, min(cols, need[slot] - (dist - 1) * cols))
                    if width > 0:
                        picks.append((slot, start, width))
                        start += width
                if picks and (dist < half or sign == 1):
                    self.moves[dist, sign] = picks
        self.margin = max(need[0], need[rows + 1])
        self.margin_blocks = -(-self.margin // cols)

    def payload(self, move):
        _, start, width = self.moves[move][-1]
        return start + width

    def span(self, slot):
        blocks = self.blocks[slot]
        if blocks == self.half:
            return 0, self.lon_total
        return (self.half - 1 - blocks) * self.cols, (2 * blocks + 1) * self.cols

    def taps_width(self, slot):
        return -(-len(self.sources(slot)) * self.span(slot)[1] // lanes) * lanes

    def taps_size(self, slot):
        count = self.span(slot)[1]
        return count if count == self.lon_total else self.taps_width(slot)

    def sources(self, slot):
        return [s for s in (slot, slot + 1, slot + 2) if s > 0 or self.outer]


def is_south(plan):
    return lax.axis_index("lat") >= plan.lat_shards // 2


def row_of(plan, south, slot):
    return jnp.where(south, plan.rows - slot, slot - 1)


def pack_body(plan, moves, x_ref, *outs):
    south = is_south(plan)
    for move, out in zip(moves, outs):
        for slot, start, width in plan.moves[move]:
            block = x_ref[row_of(plan, south, slot)]
            block = block[:width] if move[1] == 1 else block[plan.cols - width :]
            out[start : start + width] = block


def pack(plan, moves, x):
    return pl.pallas_call(
        functools.partial(pack_body, plan, moves),
        out_shape=[jax.ShapeDtypeStruct((plan.payload(m), x.shape[2]), x.dtype) for m in moves],
        in_specs=[vmem],
        out_specs=[vmem] * len(moves),
        compiler_params=pltpu.CompilerParams(vmem_limit_bytes=8 * mib),
        name="pack_columns",
    )(x)


def strip_of(plan, slot, south, x_ref, got):
    parts = [x_ref[row_of(plan, south, slot)]]
    for dist in range(1, plan.margin_blocks + 1):
        width = min(plan.cols, plan.margin - (dist - 1) * plan.cols)
        for sign in (1, -1):
            (pick,) = [p for p in plan.moves[dist, sign] if p[0] == slot]
            _, start, held = pick
            if sign == 1:
                parts.append(got[dist, sign][start : start + width])
            else:
                parts.insert(0, got[dist, sign][start + held - width : start + held])
    return jnp.concatenate(parts, axis=0)


def strip_body(plan, moves, x_ref, *refs):
    got = dict(zip(moves, refs))
    outs = refs[len(moves) :]
    south = is_south(plan)
    inner = strip_of(plan, plan.rows, south, x_ref, got)
    if not plan.outer:
        outs[0][...] = inner
        return
    outer = strip_of(plan, 1, south, x_ref, got)
    outs[0][...] = jnp.where(south, outer, inner)
    outs[1][...] = jnp.where(south, inner, outer)


def edge_rows(plan, x, got):
    moves = [m for m in plan.moves if m[0] <= plan.margin_blocks]
    count = 2 if plan.outer else 1
    size = plan.cols + 2 * plan.margin
    strips = pl.pallas_call(
        functools.partial(strip_body, plan, moves),
        out_shape=[jax.ShapeDtypeStruct((size, x.shape[2]), x.dtype)] * count,
        in_specs=[vmem] * (1 + len(moves)),
        out_specs=[vmem] * count,
        compiler_params=pltpu.CompilerParams(vmem_limit_bytes=8 * mib),
        name="pack_edge_row",
    )(x, *[got[m] for m in moves])
    if not plan.outer:
        return [lax.ppermute(strips[0], "lat", [(0, 1), (1, 0)])]
    forward = [(i, i + 1) for i in range(plan.lat_shards - 1)]
    low = lax.ppermute(strips[0], "lat", forward)
    high = lax.ppermute(strips[1], "lat", [(b, a) for a, b in forward])
    return [low, high]


def taps_body(plan, entries, lift_hbm, place_hbm, weight_hbm, out, *scratch):
    held, sem = scratch[:3], scratch[3]
    copies = [
        pltpu.make_async_copy(source, target, sem.at[order])
        for order, (source, target) in enumerate(zip((lift_hbm, place_hbm, weight_hbm), held))
    ]
    for copy in copies:
        copy.start()
    size, lat_total = lift_hbm.shape
    cols, width = plan.cols, out.shape[2]
    south = is_south(plan)
    row_start = lax.axis_index("lat") * plan.rows
    source_row = lax.broadcasted_iota(jnp.int32, (lat_total, lanes), 0)
    spots = {}
    for span in {plan.taps_size(slot) for slot in range(plan.rows)}:
        spot = lax.broadcasted_iota(jnp.int32, (size, span), 1)
        early = lax.broadcasted_iota(jnp.int32, (size, span), 0) // entries * cols
        spots[span] = lax.rem(spot + early, span)
    tall = size // entries * cols
    basis_row = lax.broadcasted_iota(jnp.int32, (tall, size), 0) // cols
    basis_col = lax.broadcasted_iota(jnp.int32, (tall, size), 1) // entries
    gather = jnp.where(basis_row == basis_col, 1.0, 0.0).astype(jnp.bfloat16)
    for copy in copies:
        copy.wait()
    tables = [ref[...].astype(jnp.bfloat16) for ref in held]
    for slot in range(plan.rows):
        first, count = plan.span(slot)
        center = (plan.half - 1) * cols - first
        here = source_row == row_start + row_of(plan, south, slot + 1)
        here = jnp.where(here, 1.0, 0.0).astype(jnp.bfloat16)
        lift, place, weight = [
            jnp.dot(table, here, preferred_element_type=jnp.float32) for table in tables
        ]
        lift = jnp.where(south, -lift, lift).astype(jnp.int32)
        place = place.astype(jnp.int32) + center
        sources = plan.sources(slot)
        span = plan.taps_size(slot)
        if count == plan.lon_total:
            place = jnp.where(place < 0, place + count, place)
            pieces = [(source - slot - 1, order * count) for order, source in enumerate(sources)]
        else:
            place = place + (lift + slot + 1 - sources[0]) * count
            pieces = [(None, 0)]
        place, weight, lift = [
            jnp.concatenate([v] * (span // lanes), axis=1) for v in (place, weight, lift)
        ]
        part = jnp.where(spots[span] == place, weight, 0.0)
        for offset, start in pieces:
            chosen = part if offset is None else jnp.where(lift == offset, part, 0.0)
            taps = jnp.dot(
                gather, chosen.astype(jnp.bfloat16), preferred_element_type=jnp.float32
            )
            taps = pltpu.roll(taps, 0, 1, stride=1, stride_axis=0)
            out[slot, :, start : start + span] = taps.astype(jnp.bfloat16)


def make_taps(plan, support):
    kinds, _, entries = support[0].shape
    width = max(plan.taps_width(slot) for slot in range(plan.rows))
    tables = [s.transpose(0, 2, 1).reshape(kinds * entries, -1) for s in support]
    scratch = [pltpu.VMEM(t.shape, t.dtype) for t in tables]
    tables = [pltpu.with_memory_space_constraint(t, pltpu.HBM) for t in tables]
    return pl.pallas_call(
        functools.partial(taps_body, plan, entries),
        out_shape=jax.ShapeDtypeStruct((plan.rows, kinds * plan.cols, width), jnp.bfloat16),
        in_specs=[pl.BlockSpec(memory_space=pltpu.HBM)] * 3,
        out_specs=vmem,
        scratch_shapes=scratch + [pltpu.SemaphoreType.DMA((3,))],
        compiler_params=pltpu.CompilerParams(vmem_limit_bytes=8 * mib),
        cost_estimate=pl.CostEstimate(flops=3 * 10**9, bytes_accessed=10**7, transcendentals=0),
        name="filter_taps",
    )(*tables)


def fill_window(plan, sources, south, x_ref, got, edges, win):
    rows, cols = plan.rows, plan.cols
    middle = (plan.half - 1) * cols
    for slot in sources:
        if slot in (0, rows + 1):
            strip = edges[0][...]
            if plan.outer:
                first, last = (edges[1], edges[0]) if slot == 0 else (edges[0], edges[1])
                strip = jnp.where(south, first[...], last[...])
            gap = plan.margin_blocks * cols - plan.margin
            if gap > 0:
                gap = jnp.zeros((gap, strip.shape[1]), strip.dtype)
                strip = jnp.concatenate([gap, strip, gap], axis=0)
            start = middle - plan.margin_blocks * cols
            win[sources.index(slot), start : start + strip.shape[0]] = strip
        else:
            win[sources.index(slot), middle : middle + cols] = x_ref[row_of(plan, south, slot)]
    for (dist, sign), ref in got.items():
        place = middle + sign * dist * cols
        for slot, start, width in plan.moves[dist, sign]:
            if slot not in sources:
                continue
            block = ref[start : start + width]
            if width < cols:
                gap = jnp.zeros((cols - width, block.shape[1]), block.dtype)
                block = jnp.concatenate([block, gap] if sign == 1 else [gap, block], axis=0)
            win[sources.index(slot), place : place + cols] = block


def compute_body(plan, slots, moves, edge_count, chained, *refs):
    x_ref = refs[0]
    got = dict(zip(moves, refs[1:]))
    used = 1 + len(moves)
    edges = refs[used : used + edge_count]
    used += edge_count
    taps_ref, mix_ref, gain_ref, up_ref, down_ref = refs[used : used + 5]
    used += 5 + chained
    out_ref, win, response, result, sem = refs[used:]
    rows, cols = plan.rows, plan.cols
    channels = x_ref.shape[2]
    kinds = mix_ref.shape[0] // channels
    south = is_south(plan)
    middle = (plan.half - 1) * cols
    sources = sorted({s for slot in slots for s in plan.sources(slot)})
    fill_window(plan, sources, south, x_ref, got, edges, win)
    for order, slot in enumerate(slots):
        first, count = plan.span(slot)
        found = [win[sources.index(s), first : first + count] for s in plan.sources(slot)]
        total = jnp.dot(
            taps_ref[slot, :, : count * len(found)],
            jnp.concatenate(found, axis=0),
            preferred_element_type=jnp.float32,
        )
        total = total.astype(jnp.bfloat16)
        for kind in range(kinds):
            place = slice(order * cols, (order + 1) * cols)
            depth = slice(kind * channels, (kind + 1) * channels)
            response[place, depth] = total[kind * cols : (kind + 1) * cols]
    mixed = jnp.dot(response[...], mix_ref[...], preferred_element_type=jnp.float32)
    own = [win[sources.index(slot + 1), middle : middle + cols] for slot in slots]
    latent = jnp.concatenate(own, axis=0).astype(jnp.float32) + mixed
    mean = jnp.mean(latent, axis=1, keepdims=True)
    variance = jnp.mean(jnp.square(latent - mean), axis=1, keepdims=True)
    normed = (latent - mean) * lax.rsqrt(variance + norm_eps) * gain_ref[...]
    hidden = jnp.dot(normed.astype(jnp.bfloat16), up_ref[...], preferred_element_type=jnp.float32)
    hidden = (0.5 * hidden * (1.0 + lax.erf(hidden * 0.5**0.5))).astype(jnp.bfloat16)
    output = latent + jnp.dot(hidden, down_ref[...], preferred_element_type=jnp.float32)
    output = output.astype(jnp.bfloat16)
    copies = []
    for number, (offset, run) in enumerate(runs_of(slots)):
        size = len(run)
        for order in range(size):
            spot = offset + jnp.where(south, size - 1 - order, order)
            place = (offset + order) * cols
            result[spot] = output[place : place + cols]
        first_row = jnp.where(south, rows - 1 - run[-1], run[0])
        source = result.at[pl.ds(offset, size)]
        target = out_ref.at[pl.ds(first_row, size)]
        copies.append(pltpu.make_async_copy(source, target, sem.at[number]))
        copies[-1].start()
    for copy in copies:
        copy.wait()


def runs_of(slots):
    runs = []
    for position, slot in enumerate(slots):
        if runs and runs[-1][1][-1] + 1 == slot:
            runs[-1][1].append(slot)
        else:
            runs.append((position, [slot]))
    return runs


def compute(plan, slots, x, got, edges, taps, weights, chain):
    sources = sorted({s for slot in slots for s in plan.sources(slot)})
    moves = [m for m, picks in plan.moves.items() if any(p[0] in sources for p in picks)]
    reach = max(plan.blocks[slot] for slot in slots)
    moves = [m for m in moves if m[0] <= reach]
    edges = edges if set(sources) & {0, plan.rows + 1} else []
    args = [x, *[got[m] for m in moves], *edges, taps, *weights]
    specs = [vmem] * len(args)
    if chain is not None:
        args.append(chain)
        specs.append(anywhere)
    channels = x.shape[2]
    depth = weights[0].shape[0]
    return pl.pallas_call(
        functools.partial(compute_body, plan, slots, moves, len(edges), chain is not None),
        out_shape=jax.ShapeDtypeStruct(x.shape, x.dtype),
        in_specs=specs,
        out_specs=anywhere,
        scratch_shapes=[
            pltpu.VMEM((len(sources), plan.lon_total, channels), x.dtype),
            pltpu.VMEM((len(slots) * plan.cols, depth), x.dtype),
            pltpu.VMEM((len(slots), plan.cols, channels), x.dtype),
            pltpu.SemaphoreType.DMA((len(runs_of(slots)),)),
        ],
        input_output_aliases={} if chain is None else {len(args) - 1: 0},
        compiler_params=pltpu.CompilerParams(vmem_limit_bytes=24 * mib),
        cost_estimate=pl.CostEstimate(flops=10**6, bytes_accessed=10**5, transcendentals=0),
        name="filter_mix_mlp",
    )(*args)


def on_device(
    fields,
    support_rows,
    support_lons,
    support_weights,
    mix_weight,
    norm_gain,
    up_weight,
    down_weight,
):
    channels, rows, cols = fields.shape
    count = lax.axis_size("lon")
    plan = Plan(rows, cols, lax.axis_size("lat"), count)
    half = plan.half
    x = jnp.transpose(fields, (1, 2, 0))

    direct = [m for m in plan.moves if m[0] < half - 1 or m[0] == half]
    close = [m for m in direct if m[0] == 1]
    wide = [m for m in direct if m[0] > 1]
    sent = dict(zip(close, pack(plan, close, x)))
    later, sent[1, 1], sent[1, -1] = lax.optimization_barrier((x, sent[1, 1], sent[1, -1]))
    sent.update(zip(wide, pack(plan, wide, later)))

    def shifted(value, step):
        return lax.ppermute(value, "lon", [((i + step) % count, i) for i in range(count)])

    got = {m: shifted(sent[m], m[0] * m[1]) for m in direct}
    forward = (half - 1, 1) in plan.moves and half > 2
    if forward:
        got[half - 1, 1] = shifted(got[half, 1], -1)
    taps = make_taps(plan, (support_rows, support_lons, support_weights))
    if forward:
        opposite, taps = lax.optimization_barrier((got[half, 1], taps))
        got[half - 1, -1] = shifted(opposite, 1)
    first = [m for m in got if m[0] <= plan.margin_blocks]
    joined, taps = lax.optimization_barrier(([got[m] for m in first], taps))
    got.update(zip(first, joined))
    edges = edge_rows(plan, x, got)
    weights = (mix_weight.reshape(-1, channels), norm_gain[None], up_weight, down_weight)
    inner = range(1 if plan.outer else 0, rows - 1)
    near = [slot for slot in inner if plan.blocks[slot] <= 1]
    far = [slot for slot in range(rows) if slot not in near]
    output = None
    for slots in (near, far):
        if slots:
            output = compute(plan, slots, x, got, edges, taps, weights, output)
    return jnp.transpose(output, (2, 0, 1))


def solution(mesh):
    in_specs = (P("member", "lat", "lon"), P(), P(), P(), P(), P(), P(), P())
    out_specs = P("member", "lat", "lon")
    return jax.shard_map(
        on_device, mesh=mesh, in_specs=in_specs, out_specs=out_specs, check_vma=False
    )
```

```python
import functools

import jax
import jax.numpy as jnp
from jax import lax
from jax.experimental import pallas as pl
from jax.experimental.pallas import tpu as pltpu
from jax.sharding import PartitionSpec as P

norm_eps = 1e-05
lanes = 128
mib = 2**20
vmem = pl.BlockSpec(memory_space=pltpu.VMEM)
anywhere = pl.BlockSpec(memory_space=pl.ANY)


class Plan:
    def __init__(self, rows, cols, lat_shards, lon_shards):
        self.rows, self.cols = rows, cols
        self.lat_shards, self.lon_shards = lat_shards, lon_shards
        lat_total, lon_total = rows * lat_shards, cols * lon_shards
        self.lon_total = lon_total
        self.half = half = lon_shards // 2
        self.outer = lat_shards > 2
        reach = [0] * rows
        need = [0] * (rows + 2)
        for shard in range(lat_shards // 2):
            for slot in range(rows):
                row = shard * rows + slot
                span = min(lon_total // 2, 4 * lat_total // min(row + 1, lat_total - row))
                reach[slot] = max(reach[slot], span)
                for source in (slot, slot + 1, slot + 2):
                    if shard > 0 or source > 0:
                        need[source] = max(need[source], span)
        self.blocks = [min(half, -(-span // cols)) for span in reach]
        self.moves = {}
        for dist in range(1, half + 1):
            for sign in (1, -1):
                picks, start = [], 0
                for slot in range(1, rows + 1):
                    if dist >= half - 1:
                        width = cols if need[slot] > (half - 2) * cols else 0
                    else:
                        width = max(0, min(cols, need[slot] - (dist - 1) * cols))
                    if width > 0:
                        picks.append((slot, start, width))
                        start += width
                if picks and (dist < half or sign == 1):
                    self.moves[dist, sign] = picks
        self.margin = max(need[0], need[rows + 1])
        self.margin_blocks = -(-self.margin // cols)

    def payload(self, move):
        _, start, width = self.moves[move][-1]
        return start + width

    def span(self, slot):
        blocks = self.blocks[slot]
        if blocks == self.half:
            return 0, self.lon_total
        return (self.half - 1 - blocks) * self.cols, (2 * blocks + 1) * self.cols

    def taps_width(self, slot):
        return -(-len(self.sources(slot)) * self.span(slot)[1] // lanes) * lanes

    def taps_size(self, slot):
        count = self.span(slot)[1]
        return count if count == self.lon_total else self.taps_width(slot)

    def sources(self, slot):
        return [s for s in (slot, slot + 1, slot + 2) if s > 0 or self.outer]


def is_south(plan):
    return lax.axis_index("lat") >= plan.lat_shards // 2


def row_of(plan, south, slot):
    return jnp.where(south, plan.rows - slot, slot - 1)


def pack_body(plan, moves, x_ref, *outs):
    south = is_south(plan)
    for move, out in zip(moves, outs):
        for slot, start, width in plan.moves[move]:
            block = x_ref[row_of(plan, south, slot)]
            block = block[:width] if move[1] == 1 else block[plan.cols - width :]
            out[start : start + width] = block


def pack(plan, moves, x):
    return pl.pallas_call(
        functools.partial(pack_body, plan, moves),
        out_shape=[jax.ShapeDtypeStruct((plan.payload(m), x.shape[2]), x.dtype) for m in moves],
        in_specs=[vmem],
        out_specs=[vmem] * len(moves),
        compiler_params=pltpu.CompilerParams(vmem_limit_bytes=8 * mib),
        name="pack_columns",
    )(x)


def strip_of(plan, slot, south, x_ref, got):
    parts = [x_ref[row_of(plan, south, slot)]]
    for dist in range(1, plan.margin_blocks + 1):
        width = min(plan.cols, plan.margin - (dist - 1) * plan.cols)
        for sign in (1, -1):
            (pick,) = [p for p in plan.moves[dist, sign] if p[0] == slot]
            _, start, held = pick
            if sign == 1:
                parts.append(got[dist, sign][start : start + width])
            else:
                parts.insert(0, got[dist, sign][start + held - width : start + held])
    return jnp.concatenate(parts, axis=0)


def strip_body(plan, moves, x_ref, *refs):
    got = dict(zip(moves, refs))
    outs = refs[len(moves) :]
    south = is_south(plan)
    inner = strip_of(plan, plan.rows, south, x_ref, got)
    if not plan.outer:
        outs[0][...] = inner
        return
    outer = strip_of(plan, 1, south, x_ref, got)
    outs[0][...] = jnp.where(south, outer, inner)
    outs[1][...] = jnp.where(south, inner, outer)


def edge_rows(plan, x, got):
    moves = [m for m in plan.moves if m[0] <= plan.margin_blocks]
    count = 2 if plan.outer else 1
    size = plan.cols + 2 * plan.margin
    strips = pl.pallas_call(
        functools.partial(strip_body, plan, moves),
        out_shape=[jax.ShapeDtypeStruct((size, x.shape[2]), x.dtype)] * count,
        in_specs=[vmem] * (1 + len(moves)),
        out_specs=[vmem] * count,
        compiler_params=pltpu.CompilerParams(vmem_limit_bytes=8 * mib),
        name="pack_edge_row",
    )(x, *[got[m] for m in moves])
    if not plan.outer:
        return [lax.ppermute(strips[0], "lat", [(0, 1), (1, 0)])]
    forward = [(i, i + 1) for i in range(plan.lat_shards - 1)]
    low = lax.ppermute(strips[0], "lat", forward)
    high = lax.ppermute(strips[1], "lat", [(b, a) for a, b in forward])
    return [low, high]


def taps_body(plan, entries, lift_hbm, place_hbm, weight_hbm, out, *scratch):
    held, sem = scratch[:3], scratch[3]
    copies = [
        pltpu.make_async_copy(source, target, sem.at[order])
        for order, (source, target) in enumerate(zip((lift_hbm, place_hbm, weight_hbm), held))
    ]
    for copy in copies:
        copy.start()
    size, lat_total = lift_hbm.shape
    cols, width = plan.cols, out.shape[2]
    south = is_south(plan)
    row_start = lax.axis_index("lat") * plan.rows
    source_row = lax.broadcasted_iota(jnp.int32, (lat_total, lanes), 0)
    spots = {}
    for span in {plan.taps_size(slot) for slot in range(plan.rows)}:
        spot = lax.broadcasted_iota(jnp.int32, (size, span), 1)
        early = lax.broadcasted_iota(jnp.int32, (size, span), 0) // entries * cols
        spots[span] = lax.rem(spot + early, span)
    tall = size // entries * cols
    basis_row = lax.broadcasted_iota(jnp.int32, (tall, size), 0) // cols
    basis_col = lax.broadcasted_iota(jnp.int32, (tall, size), 1) // entries
    gather = jnp.where(basis_row == basis_col, 1.0, 0.0).astype(jnp.bfloat16)
    for copy in copies:
        copy.wait()
    tables = [ref[...].astype(jnp.bfloat16) for ref in held]
    for slot in range(plan.rows):
        first, count = plan.span(slot)
        center = (plan.half - 1) * cols - first
        here = source_row == row_start + row_of(plan, south, slot + 1)
        here = jnp.where(here, 1.0, 0.0).astype(jnp.bfloat16)
        lift, place, weight = [
            jnp.dot(table, here, preferred_element_type=jnp.float32) for table in tables
        ]
        lift = jnp.where(south, -lift, lift).astype(jnp.int32)
        place = place.astype(jnp.int32) + center
        sources = plan.sources(slot)
        span = plan.taps_size(slot)
        if count == plan.lon_total:
            place = jnp.where(place < 0, place + count, place)
            pieces = [(source - slot - 1, order * count) for order, source in enumerate(sources)]
        else:
            place = place + (lift + slot + 1 - sources[0]) * count
            pieces = [(None, 0)]
        place, weight, lift = [
            jnp.concatenate([v] * (span // lanes), axis=1) for v in (place, weight, lift)
        ]
        part = jnp.where(spots[span] == place, weight, 0.0)
        for offset, start in pieces:
            chosen = part if offset is None else jnp.where(lift == offset, part, 0.0)
            taps = jnp.dot(
                gather, chosen.astype(jnp.bfloat16), preferred_element_type=jnp.float32
            )
            taps = pltpu.roll(taps, 0, 1, stride=1, stride_axis=0)
            out[slot, :, start : start + span] = taps.astype(jnp.bfloat16)


def make_taps(plan, support):
    kinds, _, entries = support[0].shape
    width = max(plan.taps_width(slot) for slot in range(plan.rows))
    tables = [s.transpose(0, 2, 1).reshape(kinds * entries, -1) for s in support]
    scratch = [pltpu.VMEM(t.shape, t.dtype) for t in tables]
    tables = [pltpu.with_memory_space_constraint(t, pltpu.HBM) for t in tables]
    return pl.pallas_call(
        functools.partial(taps_body, plan, entries),
        out_shape=jax.ShapeDtypeStruct((plan.rows, kinds * plan.cols, width), jnp.bfloat16),
        in_specs=[pl.BlockSpec(memory_space=pltpu.HBM)] * 3,
        out_specs=vmem,
        scratch_shapes=scratch + [pltpu.SemaphoreType.DMA((3,))],
        compiler_params=pltpu.CompilerParams(vmem_limit_bytes=8 * mib),
        cost_estimate=pl.CostEstimate(flops=3 * 10**9, bytes_accessed=10**7, transcendentals=0),
        name="filter_taps",
    )(*tables)


def fill_window(plan, sources, south, x_ref, got, edges, win):
    rows, cols = plan.rows, plan.cols
    middle = (plan.half - 1) * cols
    for slot in sources:
        if slot in (0, rows + 1):
            strip = edges[0][...]
            if plan.outer:
                first, last = (edges[1], edges[0]) if slot == 0 else (edges[0], edges[1])
                strip = jnp.where(south, first[...], last[...])
            gap = plan.margin_blocks * cols - plan.margin
            if gap > 0:
                gap = jnp.zeros((gap, strip.shape[1]), strip.dtype)
                strip = jnp.concatenate([gap, strip, gap], axis=0)
            start = middle - plan.margin_blocks * cols
            users = [s for s in range(rows) if slot in plan.sources(s)]
            if max(plan.blocks[s] for s in users) > plan.margin_blocks:
                win[sources.index(slot)] = jnp.zeros(win.shape[1:], win.dtype)
            win[sources.index(slot), start : start + strip.shape[0]] = strip
        else:
            win[sources.index(slot), middle : middle + cols] = x_ref[row_of(plan, south, slot)]
    for (dist, sign), ref in got.items():
        place = middle + sign * dist * cols
        for slot, start, width in plan.moves[dist, sign]:
            if slot not in sources:
                continue
            block = ref[start : start + width]
            if width < cols:
                gap = jnp.zeros((cols - width, block.shape[1]), block.dtype)
                block = jnp.concatenate([block, gap] if sign == 1 else [gap, block], axis=0)
            win[sources.index(slot), place : place + cols] = block


def compute_body(plan, slots, moves, edge_count, chained, *refs):
    x_ref = refs[0]
    got = dict(zip(moves, refs[1:]))
    used = 1 + len(moves)
    edges = refs[used : used + edge_count]
    used += edge_count
    taps_ref, mix_ref, gain_ref, up_ref, down_ref = refs[used : used + 5]
    used += 5 + chained
    out_ref, win, response, result, sem = refs[used:]
    rows, cols = plan.rows, plan.cols
    channels = x_ref.shape[2]
    kinds = mix_ref.shape[0] // channels
    south = is_south(plan)
    middle = (plan.half - 1) * cols
    sources = sorted({s for slot in slots for s in plan.sources(slot)})
    fill_window(plan, sources, south, x_ref, got, edges, win)
    for order, slot in enumerate(slots):
        first, count = plan.span(slot)
        found = [win[sources.index(s), first : first + count] for s in plan.sources(slot)]
        total = jnp.dot(
            taps_ref[slot, :, : count * len(found)],
            jnp.concatenate(found, axis=0),
            preferred_element_type=jnp.float32,
        )
        total = total.astype(jnp.bfloat16)
        for kind in range(kinds):
            place = slice(order * cols, (order + 1) * cols)
            depth = slice(kind * channels, (kind + 1) * channels)
            response[place, depth] = total[kind * cols : (kind + 1) * cols]
    mixed = jnp.dot(response[...], mix_ref[...], preferred_element_type=jnp.float32)
    own = [win[sources.index(slot + 1), middle : middle + cols] for slot in slots]
    latent = jnp.concatenate(own, axis=0).astype(jnp.float32) + mixed
    mean = jnp.mean(latent, axis=1, keepdims=True)
    variance = jnp.mean(jnp.square(latent - mean), axis=1, keepdims=True)
    normed = (latent - mean) * lax.rsqrt(variance + norm_eps) * gain_ref[...]
    hidden = jnp.dot(normed.astype(jnp.bfloat16), up_ref[...], preferred_element_type=jnp.float32)
    hidden = (0.5 * hidden * (1.0 + lax.erf(hidden * 0.5**0.5))).astype(jnp.bfloat16)
    output = latent + jnp.dot(hidden, down_ref[...], preferred_element_type=jnp.float32)
    output = output.astype(jnp.bfloat16)
    copies = []
    for number, (offset, run) in enumerate(runs_of(slots)):
        size = len(run)
        for order in range(size):
            spot = offset + jnp.where(south, size - 1 - order, order)
            place = (offset + order) * cols
            result[spot] = output[place : place + cols]
        first_row = jnp.where(south, rows - 1 - run[-1], run[0])
        source = result.at[pl.ds(offset, size)]
        target = out_ref.at[pl.ds(first_row, size)]
        copies.append(pltpu.make_async_copy(source, target, sem.at[number]))
        copies[-1].start()
    for copy in copies:
        copy.wait()


def runs_of(slots):
    runs = []
    for position, slot in enumerate(slots):
        if runs and runs[-1][1][-1] + 1 == slot:
            runs[-1][1].append(slot)
        else:
            runs.append((position, [slot]))
    return runs


def compute(plan, slots, x, got, edges, taps, weights, chain):
    sources = sorted({s for slot in slots for s in plan.sources(slot)})
    moves = [m for m, picks in plan.moves.items() if any(p[0] in sources for p in picks)]
    reach = max(plan.blocks[slot] for slot in slots)
    moves = [m for m in moves if m[0] <= reach]
    edges = edges if set(sources) & {0, plan.rows + 1} else []
    args = [x, *[got[m] for m in moves], *edges, taps, *weights]
    specs = [vmem] * len(args)
    if chain is not None:
        args.append(chain)
        specs.append(anywhere)
    channels = x.shape[2]
    depth = weights[0].shape[0]
    return pl.pallas_call(
        functools.partial(compute_body, plan, slots, moves, len(edges), chain is not None),
        out_shape=jax.ShapeDtypeStruct(x.shape, x.dtype),
        in_specs=specs,
        out_specs=anywhere,
        scratch_shapes=[
            pltpu.VMEM((len(sources), plan.lon_total, channels), x.dtype),
            pltpu.VMEM((len(slots) * plan.cols, depth), x.dtype),
            pltpu.VMEM((len(slots), plan.cols, channels), x.dtype),
            pltpu.SemaphoreType.DMA((len(runs_of(slots)),)),
        ],
        input_output_aliases={} if chain is None else {len(args) - 1: 0},
        compiler_params=pltpu.CompilerParams(vmem_limit_bytes=24 * mib),
        cost_estimate=pl.CostEstimate(flops=10**6, bytes_accessed=10**5, transcendentals=0),
        name="filter_mix_mlp",
    )(*args)


def on_device(
    fields,
    support_rows,
    support_lons,
    support_weights,
    mix_weight,
    norm_gain,
    up_weight,
    down_weight,
):
    channels, rows, cols = fields.shape
    count = lax.axis_size("lon")
    plan = Plan(rows, cols, lax.axis_size("lat"), count)
    half = plan.half
    x = jnp.transpose(fields, (1, 2, 0))

    direct = [m for m in plan.moves if m[0] < half - 1 or m[0] == half]
    close = [m for m in direct if m[0] == 1]
    wide = [m for m in direct if m[0] > 1]
    sent = dict(zip(close, pack(plan, close, x)))
    later, sent[1, 1], sent[1, -1] = lax.optimization_barrier((x, sent[1, 1], sent[1, -1]))
    sent.update(zip(wide, pack(plan, wide, later)))

    def shifted(value, step):
        return lax.ppermute(value, "lon", [((i + step) % count, i) for i in range(count)])

    got = {m: shifted(sent[m], m[0] * m[1]) for m in direct}
    forward = (half - 1, 1) in plan.moves and half > 2
    if forward:
        got[half - 1, 1] = shifted(got[half, 1], -1)
    taps = make_taps(plan, (support_rows, support_lons, support_weights))
    if forward:
        opposite, taps = lax.optimization_barrier((got[half, 1], taps))
        got[half - 1, -1] = shifted(opposite, 1)
    first = [m for m in got if m[0] <= plan.margin_blocks]
    joined, taps = lax.optimization_barrier(([got[m] for m in first], taps))
    got.update(zip(first, joined))
    edges = edge_rows(plan, x, got)
    weights = (mix_weight.reshape(-1, channels), norm_gain[None], up_weight, down_weight)
    inner = range(1 if plan.outer else 0, rows - 1)
    near = [slot for slot in inner if plan.blocks[slot] <= 1]
    far = [slot for slot in range(rows) if slot not in near]
    output = None
    for slots in (near, far):
        if slots:
            output = compute(plan, slots, x, got, edges, taps, weights, output)
    return jnp.transpose(output, (2, 0, 1))


def solution(mesh):
    in_specs = (P("member", "lat", "lon"), P(), P(), P(), P(), P(), P(), P())
    out_specs = P("member", "lat", "lon")
    return jax.shard_map(
        on_device, mesh=mesh, in_specs=in_specs, out_specs=out_specs, check_vma=False
    )
```

```python
import functools

import jax
import jax.numpy as jnp
from jax import lax
from jax.experimental import pallas as pl
from jax.experimental.pallas import tpu as pltpu
from jax.sharding import PartitionSpec as P

norm_eps = 1e-05
lanes = 128
mib = 2**20
vmem = pl.BlockSpec(memory_space=pltpu.VMEM)
anywhere = pl.BlockSpec(memory_space=pl.ANY)


class Plan:
    def __init__(self, rows, cols, lat_shards, lon_shards):
        self.rows, self.cols = rows, cols
        self.lat_shards, self.lon_shards = lat_shards, lon_shards
        lat_total, lon_total = rows * lat_shards, cols * lon_shards
        self.lon_total = lon_total
        self.half = half = lon_shards // 2
        self.outer = lat_shards > 2
        reach = [0] * rows
        need = [0] * (rows + 2)
        for shard in range(lat_shards // 2):
            for slot in range(rows):
                row = shard * rows + slot
                span = min(lon_total // 2, 4 * lat_total // min(row + 1, lat_total - row))
                reach[slot] = max(reach[slot], span)
                for source in (slot, slot + 1, slot + 2):
                    if shard > 0 or source > 0:
                        need[source] = max(need[source], span)
        self.blocks = [min(half, -(-span // cols)) for span in reach]
        self.moves = {}
        for dist in range(1, half + 1):
            for sign in (1, -1):
                picks, start = [], 0
                for slot in range(1, rows + 1):
                    if dist >= half - 1:
                        width = cols if need[slot] > (half - 2) * cols else 0
                    else:
                        width = max(0, min(cols, need[slot] - (dist - 1) * cols))
                    if width > 0:
                        picks.append((slot, start, width))
                        start += width
                if picks and (dist < half or sign == 1):
                    self.moves[dist, sign] = picks
        self.margin = max(need[0], need[rows + 1])
        self.margin_blocks = -(-self.margin // cols)

    def payload(self, move):
        _, start, width = self.moves[move][-1]
        return start + width

    def span(self, slot):
        blocks = self.blocks[slot]
        if blocks == self.half:
            return 0, self.lon_total
        return (self.half - 1 - blocks) * self.cols, (2 * blocks + 1) * self.cols

    def taps_width(self, slot):
        return -(-len(self.sources(slot)) * self.span(slot)[1] // lanes) * lanes

    def taps_size(self, slot):
        count = self.span(slot)[1]
        return count if count == self.lon_total else self.taps_width(slot)

    def sources(self, slot):
        return [s for s in (slot, slot + 1, slot + 2) if s > 0 or self.outer]


def is_south(plan):
    return lax.axis_index("lat") >= plan.lat_shards // 2


def row_of(plan, south, slot):
    return jnp.where(south, plan.rows - slot, slot - 1)


def pack_body(plan, moves, x_ref, *outs):
    south = is_south(plan)
    for move, out in zip(moves, outs):
        for slot, start, width in plan.moves[move]:
            block = x_ref[row_of(plan, south, slot)]
            block = block[:width] if move[1] == 1 else block[plan.cols - width :]
            out[start : start + width] = block


def pack(plan, moves, x):
    return pl.pallas_call(
        functools.partial(pack_body, plan, moves),
        out_shape=[jax.ShapeDtypeStruct((plan.payload(m), x.shape[2]), x.dtype) for m in moves],
        in_specs=[vmem],
        out_specs=[vmem] * len(moves),
        compiler_params=pltpu.CompilerParams(vmem_limit_bytes=8 * mib),
        name="pack_columns",
    )(x)


def strip_of(plan, slot, south, x_ref, got):
    parts = [x_ref[row_of(plan, south, slot)]]
    for dist in range(1, plan.margin_blocks + 1):
        width = min(plan.cols, plan.margin - (dist - 1) * plan.cols)
        for sign in (1, -1):
            (pick,) = [p for p in plan.moves[dist, sign] if p[0] == slot]
            _, start, held = pick
            if sign == 1:
                parts.append(got[dist, sign][start : start + width])
            else:
                parts.insert(0, got[dist, sign][start + held - width : start + held])
    return jnp.concatenate(parts, axis=0)


def strip_body(plan, moves, x_ref, *refs):
    got = dict(zip(moves, refs))
    outs = refs[len(moves) :]
    south = is_south(plan)
    inner = strip_of(plan, plan.rows, south, x_ref, got)
    if not plan.outer:
        outs[0][...] = inner
        return
    outer = strip_of(plan, 1, south, x_ref, got)
    outs[0][...] = jnp.where(south, outer, inner)
    outs[1][...] = jnp.where(south, inner, outer)


def edge_rows(plan, x, got):
    moves = [m for m in plan.moves if m[0] <= plan.margin_blocks]
    count = 2 if plan.outer else 1
    size = plan.cols + 2 * plan.margin
    strips = pl.pallas_call(
        functools.partial(strip_body, plan, moves),
        out_shape=[jax.ShapeDtypeStruct((size, x.shape[2]), x.dtype)] * count,
        in_specs=[vmem] * (1 + len(moves)),
        out_specs=[vmem] * count,
        compiler_params=pltpu.CompilerParams(vmem_limit_bytes=8 * mib),
        name="pack_edge_row",
    )(x, *[got[m] for m in moves])
    if not plan.outer:
        return [lax.ppermute(strips[0], "lat", [(0, 1), (1, 0)])]
    forward = [(i, i + 1) for i in range(plan.lat_shards - 1)]
    low = lax.ppermute(strips[0], "lat", forward)
    high = lax.ppermute(strips[1], "lat", [(b, a) for a, b in forward])
    return [low, high]


def taps_body(plan, entries, lift_hbm, place_hbm, weight_hbm, out, *scratch):
    held, sem = scratch[:3], scratch[3]
    copies = [
        pltpu.make_async_copy(source, target, sem.at[order])
        for order, (source, target) in enumerate(zip((lift_hbm, place_hbm, weight_hbm), held))
    ]
    for copy in copies:
        copy.start()
    size, lat_total = lift_hbm.shape
    cols, width = plan.cols, out.shape[2]
    south = is_south(plan)
    row_start = lax.axis_index("lat") * plan.rows
    source_row = lax.broadcasted_iota(jnp.int32, (lat_total, lanes), 0)
    spots = {}
    for span in {plan.taps_size(slot) for slot in range(plan.rows)}:
        spot = lax.broadcasted_iota(jnp.int32, (size, span), 1)
        early = lax.broadcasted_iota(jnp.int32, (size, span), 0) // entries * cols
        spots[span] = lax.rem(spot + early, span)
    tall = size // entries * cols
    basis_row = lax.broadcasted_iota(jnp.int32, (tall, size), 0) // cols
    basis_col = lax.broadcasted_iota(jnp.int32, (tall, size), 1) // entries
    gather = jnp.where(basis_row == basis_col, 1.0, 0.0).astype(jnp.bfloat16)
    for copy in copies:
        copy.wait()
    tables = [ref[...].astype(jnp.bfloat16) for ref in held]
    for slot in range(plan.rows):
        first, count = plan.span(slot)
        center = (plan.half - 1) * cols - first
        here = source_row == row_start + row_of(plan, south, slot + 1)
        here = jnp.where(here, 1.0, 0.0).astype(jnp.bfloat16)
        lift, place, weight = [
            jnp.dot(table, here, preferred_element_type=jnp.float32) for table in tables
        ]
        lift = jnp.where(south, -lift, lift).astype(jnp.int32)
        place = place.astype(jnp.int32) + center
        sources = plan.sources(slot)
        span = plan.taps_size(slot)
        if count == plan.lon_total:
            place = jnp.where(place < 0, place + count, place)
            pieces = [(source - slot - 1, order * count) for order, source in enumerate(sources)]
        else:
            place = place + (lift + slot + 1 - sources[0]) * count
            pieces = [(None, 0)]
        place, weight, lift = [
            jnp.concatenate([v] * (span // lanes), axis=1) for v in (place, weight, lift)
        ]
        part = jnp.where(spots[span] == place, weight, 0.0)
        for offset, start in pieces:
            chosen = part if offset is None else jnp.where(lift == offset, part, 0.0)
            taps = jnp.dot(
                gather, chosen.astype(jnp.bfloat16), preferred_element_type=jnp.float32
            )
            taps = pltpu.roll(taps, 0, 1, stride=1, stride_axis=0)
            out[slot, :, start : start + span] = taps.astype(jnp.bfloat16)


def make_taps(plan, support):
    kinds, _, entries = support[0].shape
    width = max(plan.taps_width(slot) for slot in range(plan.rows))
    tables = [s.transpose(0, 2, 1).reshape(kinds * entries, -1) for s in support]
    scratch = [pltpu.VMEM(t.shape, t.dtype) for t in tables]
    tables = [pltpu.with_memory_space_constraint(t, pltpu.HBM) for t in tables]
    return pl.pallas_call(
        functools.partial(taps_body, plan, entries),
        out_shape=jax.ShapeDtypeStruct((plan.rows, kinds * plan.cols, width), jnp.bfloat16),
        in_specs=[pl.BlockSpec(memory_space=pltpu.HBM)] * 3,
        out_specs=vmem,
        scratch_shapes=scratch + [pltpu.SemaphoreType.DMA((3,))],
        compiler_params=pltpu.CompilerParams(vmem_limit_bytes=8 * mib),
        cost_estimate=pl.CostEstimate(flops=3 * 10**9, bytes_accessed=10**7, transcendentals=0),
        name="filter_taps",
    )(*tables)


def fill_window(plan, sources, south, x_ref, got, edges, win):
    rows, cols = plan.rows, plan.cols
    middle = (plan.half - 1) * cols
    for slot in sources:
        if slot in (0, rows + 1):
            strip = edges[0][...]
            if plan.outer:
                first, last = (edges[1], edges[0]) if slot == 0 else (edges[0], edges[1])
                strip = jnp.where(south, first[...], last[...])
            gap = plan.margin_blocks * cols - plan.margin
            if gap > 0:
                gap = jnp.zeros((gap, strip.shape[1]), strip.dtype)
                strip = jnp.concatenate([gap, strip, gap], axis=0)
            start = middle - plan.margin_blocks * cols
            users = [s for s in range(rows) if slot in plan.sources(s)]
            if max(plan.blocks[s] for s in users) > plan.margin_blocks:
                win[sources.index(slot)] = jnp.zeros(win.shape[1:], win.dtype)
            win[sources.index(slot), start : start + strip.shape[0]] = strip
        else:
            win[sources.index(slot), middle : middle + cols] = x_ref[row_of(plan, south, slot)]
    for (dist, sign), ref in got.items():
        place = middle + sign * dist * cols
        for slot, start, width in plan.moves[dist, sign]:
            if slot not in sources:
                continue
            block = ref[start : start + width]
            if width < cols:
                gap = jnp.zeros((cols - width, block.shape[1]), block.dtype)
                block = jnp.concatenate([block, gap] if sign == 1 else [gap, block], axis=0)
            win[sources.index(slot), place : place + cols] = block


def compute_body(plan, slots, moves, edge_count, chained, *refs):
    x_ref = refs[0]
    got = dict(zip(moves, refs[1:]))
    used = 1 + len(moves)
    edges = refs[used : used + edge_count]
    used += edge_count
    taps_ref, mix_ref, gain_ref, up_ref, down_ref = refs[used : used + 5]
    used += 5 + chained
    out_ref, win, response, result, sem = refs[used:]
    rows, cols = plan.rows, plan.cols
    channels = x_ref.shape[2]
    kinds = mix_ref.shape[0] // channels
    south = is_south(plan)
    middle = (plan.half - 1) * cols
    sources = sorted({s for slot in slots for s in plan.sources(slot)})
    fill_window(plan, sources, south, x_ref, got, edges, win)
    for order, slot in enumerate(slots):
        first, count = plan.span(slot)
        found = [win[sources.index(s), first : first + count] for s in plan.sources(slot)]
        total = jnp.dot(
            taps_ref[slot, :, : count * len(found)],
            jnp.concatenate(found, axis=0),
            preferred_element_type=jnp.float32,
        )
        total = total.astype(jnp.bfloat16)
        for kind in range(kinds):
            place = slice(order * cols, (order + 1) * cols)
            depth = slice(kind * channels, (kind + 1) * channels)
            response[place, depth] = total[kind * cols : (kind + 1) * cols]
    mixed = jnp.dot(response[...], mix_ref[...], preferred_element_type=jnp.float32)
    own = [win[sources.index(slot + 1), middle : middle + cols] for slot in slots]
    latent = jnp.concatenate(own, axis=0).astype(jnp.float32) + mixed
    mean = jnp.mean(latent, axis=1, keepdims=True)
    variance = jnp.mean(jnp.square(latent - mean), axis=1, keepdims=True)
    normed = (latent - mean) * lax.rsqrt(variance + norm_eps) * gain_ref[...]
    hidden = jnp.dot(normed.astype(jnp.bfloat16), up_ref[...], preferred_element_type=jnp.float32)
    hidden = (0.5 * hidden * (1.0 + lax.erf(hidden * 0.5**0.5))).astype(jnp.bfloat16)
    output = latent + jnp.dot(hidden, down_ref[...], preferred_element_type=jnp.float32)
    output = output.astype(jnp.bfloat16)
    copies = []
    for number, (offset, run) in enumerate(runs_of(slots)):
        size = len(run)
        for order in range(size):
            spot = offset + jnp.where(south, size - 1 - order, order)
            place = (offset + order) * cols
            result[spot] = output[place : place + cols]
        first_row = jnp.where(south, rows - 1 - run[-1], run[0])
        source = result.at[pl.ds(offset, size)]
        target = out_ref.at[pl.ds(first_row, size)]
        copies.append(pltpu.make_async_copy(source, target, sem.at[number]))
        copies[-1].start()
    for copy in copies:
        copy.wait()


def runs_of(slots):
    runs = []
    for position, slot in enumerate(slots):
        if runs and runs[-1][1][-1] + 1 == slot:
            runs[-1][1].append(slot)
        else:
            runs.append((position, [slot]))
    return runs


def compute(plan, slots, x, got, edges, taps, weights, chain):
    sources = sorted({s for slot in slots for s in plan.sources(slot)})
    moves = [m for m, picks in plan.moves.items() if any(p[0] in sources for p in picks)]
    reach = max(plan.blocks[slot] for slot in slots)
    moves = [m for m in moves if m[0] <= reach]
    edges = edges if set(sources) & {0, plan.rows + 1} else []
    args = [x, *[got[m] for m in moves], *edges, taps, *weights]
    specs = [vmem] * len(args)
    if chain is not None:
        args.append(chain)
        specs.append(anywhere)
    channels = x.shape[2]
    depth = weights[0].shape[0]
    return pl.pallas_call(
        functools.partial(compute_body, plan, slots, moves, len(edges), chain is not None),
        out_shape=jax.ShapeDtypeStruct(x.shape, x.dtype),
        in_specs=specs,
        out_specs=anywhere,
        scratch_shapes=[
            pltpu.VMEM((len(sources), plan.lon_total, channels), x.dtype),
            pltpu.VMEM((len(slots) * plan.cols, depth), x.dtype),
            pltpu.VMEM((len(slots), plan.cols, channels), x.dtype),
            pltpu.SemaphoreType.DMA((len(runs_of(slots)),)),
        ],
        input_output_aliases={} if chain is None else {len(args) - 1: 0},
        compiler_params=pltpu.CompilerParams(vmem_limit_bytes=24 * mib),
        cost_estimate=pl.CostEstimate(flops=10**6, bytes_accessed=10**5, transcendentals=0),
        name="filter_mix_mlp",
    )(*args)


def on_device(
    fields,
    support_rows,
    support_lons,
    support_weights,
    mix_weight,
    norm_gain,
    up_weight,
    down_weight,
):
    channels, rows, cols = fields.shape
    count = lax.axis_size("lon")
    plan = Plan(rows, cols, lax.axis_size("lat"), count)
    half = plan.half
    x = jnp.transpose(fields, (1, 2, 0))

    direct = [m for m in plan.moves if m[0] < half - 1 or m[0] == half]
    order = [[(1, 1)], [(half, 1)], [(1, -1)]]
    order = [[m for m in group if m in direct] for group in order]
    order.append([m for m in direct if all(m not in group for group in order)])
    sent, later = {}, x
    for group in order:
        if group:
            packed = pack(plan, group, later)
            sent.update(zip(group, packed))
            later, _ = lax.optimization_barrier((later, packed))

    def shifted(value, step):
        return lax.ppermute(value, "lon", [((i + step) % count, i) for i in range(count)])

    got = {m: shifted(sent[m], m[0] * m[1]) for m in direct}
    forward = (half - 1, 1) in plan.moves and half > 2
    if forward:
        got[half - 1, 1] = shifted(got[half, 1], -1)
    taps = make_taps(plan, (support_rows, support_lons, support_weights))
    if forward:
        opposite, taps = lax.optimization_barrier((got[half, 1], taps))
        got[half - 1, -1] = shifted(opposite, 1)
    first = [m for m in got if m[0] <= plan.margin_blocks]
    joined, taps = lax.optimization_barrier(([got[m] for m in first], taps))
    got.update(zip(first, joined))
    edges = edge_rows(plan, x, got)
    weights = (mix_weight.reshape(-1, channels), norm_gain[None], up_weight, down_weight)
    inner = range(1 if plan.outer else 0, rows - 1)
    near = [slot for slot in inner if plan.blocks[slot] <= 1]
    far = [slot for slot in range(rows) if slot not in near]
    output = None
    for slots in (near, far):
        if slots:
            output = compute(plan, slots, x, got, edges, taps, weights, output)
    return jnp.transpose(output, (2, 0, 1))


def solution(mesh):
    in_specs = (P("member", "lat", "lon"), P(), P(), P(), P(), P(), P(), P())
    out_specs = P("member", "lat", "lon")
    return jax.shard_map(
        on_device, mesh=mesh, in_specs=in_specs, out_specs=out_specs, check_vma=False
    )
```

```python
import functools

import jax
import jax.numpy as jnp
from jax import lax
from jax.experimental import pallas as pl
from jax.experimental.pallas import tpu as pltpu
from jax.sharding import PartitionSpec as P

norm_eps = 1e-05
lanes = 128
mib = 2**20
vmem = pl.BlockSpec(memory_space=pltpu.VMEM)
anywhere = pl.BlockSpec(memory_space=pl.ANY)


class Plan:
    def __init__(self, rows, cols, lat_shards, lon_shards):
        self.rows, self.cols = rows, cols
        self.lat_shards, self.lon_shards = lat_shards, lon_shards
        lat_total, lon_total = rows * lat_shards, cols * lon_shards
        self.lon_total = lon_total
        self.half = half = lon_shards // 2
        self.outer = lat_shards > 2
        reach = [0] * rows
        need = [0] * (rows + 2)
        for shard in range(lat_shards // 2):
            for slot in range(rows):
                row = shard * rows + slot
                span = min(lon_total // 2, 4 * lat_total // min(row + 1, lat_total - row))
                reach[slot] = max(reach[slot], span)
                for source in (slot, slot + 1, slot + 2):
                    if shard > 0 or source > 0:
                        need[source] = max(need[source], span)
        self.blocks = [min(half, -(-span // cols)) for span in reach]
        self.moves = {}
        for dist in range(1, half + 1):
            for sign in (1, -1):
                picks, start = [], 0
                for slot in range(1, rows + 1):
                    if dist >= half - 1:
                        width = cols if need[slot] > (half - 2) * cols else 0
                    else:
                        width = max(0, min(cols, need[slot] - (dist - 1) * cols))
                    if width > 0:
                        picks.append((slot, start, width))
                        start += width
                if picks and (dist < half or sign == 1):
                    self.moves[dist, sign] = picks
        self.margin = max(need[0], need[rows + 1])
        self.margin_blocks = -(-self.margin // cols)

    def payload(self, move):
        _, start, width = self.moves[move][-1]
        return start + width

    def span(self, slot):
        blocks = self.blocks[slot]
        if blocks == self.half:
            return 0, self.lon_total
        return (self.half - 1 - blocks) * self.cols, (2 * blocks + 1) * self.cols

    def taps_width(self, slot):
        return -(-len(self.sources(slot)) * self.span(slot)[1] // lanes) * lanes

    def taps_size(self, slot):
        count = self.span(slot)[1]
        return count if count == self.lon_total else self.taps_width(slot)

    def sources(self, slot):
        return [s for s in (slot, slot + 1, slot + 2) if s > 0 or self.outer]


def is_south(plan):
    return lax.axis_index("lat") >= plan.lat_shards // 2


def row_of(plan, south, slot):
    return jnp.where(south, plan.rows - slot, slot - 1)


def pack_body(plan, moves, x_ref, *outs):
    south = is_south(plan)
    for move, out in zip(moves, outs):
        for slot, start, width in plan.moves[move]:
            block = x_ref[row_of(plan, south, slot)]
            block = block[:width] if move[1] == 1 else block[plan.cols - width :]
            out[start : start + width] = block


def pack(plan, moves, x):
    return pl.pallas_call(
        functools.partial(pack_body, plan, moves),
        out_shape=[jax.ShapeDtypeStruct((plan.payload(m), x.shape[2]), x.dtype) for m in moves],
        in_specs=[vmem],
        out_specs=[vmem] * len(moves),
        compiler_params=pltpu.CompilerParams(vmem_limit_bytes=8 * mib),
        name="pack_columns",
    )(x)


def strip_of(plan, slot, south, x_ref, got):
    parts = [x_ref[row_of(plan, south, slot)]]
    for dist in range(1, plan.margin_blocks + 1):
        width = min(plan.cols, plan.margin - (dist - 1) * plan.cols)
        for sign in (1, -1):
            (pick,) = [p for p in plan.moves[dist, sign] if p[0] == slot]
            _, start, held = pick
            if sign == 1:
                parts.append(got[dist, sign][start : start + width])
            else:
                parts.insert(0, got[dist, sign][start + held - width : start + held])
    return jnp.concatenate(parts, axis=0)


def strip_body(plan, moves, x_ref, *refs):
    got = dict(zip(moves, refs))
    outs = refs[len(moves) :]
    south = is_south(plan)
    inner = strip_of(plan, plan.rows, south, x_ref, got)
    if not plan.outer:
        outs[0][...] = inner
        return
    outer = strip_of(plan, 1, south, x_ref, got)
    outs[0][...] = jnp.where(south, outer, inner)
    outs[1][...] = jnp.where(south, inner, outer)


def edge_rows(plan, x, got):
    moves = [m for m in plan.moves if m[0] <= plan.margin_blocks]
    count = 2 if plan.outer else 1
    size = plan.cols + 2 * plan.margin
    strips = pl.pallas_call(
        functools.partial(strip_body, plan, moves),
        out_shape=[jax.ShapeDtypeStruct((size, x.shape[2]), x.dtype)] * count,
        in_specs=[vmem] * (1 + len(moves)),
        out_specs=[vmem] * count,
        compiler_params=pltpu.CompilerParams(vmem_limit_bytes=8 * mib),
        name="pack_edge_row",
    )(x, *[got[m] for m in moves])
    if not plan.outer:
        return [lax.ppermute(strips[0], "lat", [(0, 1), (1, 0)])]
    forward = [(i, i + 1) for i in range(plan.lat_shards - 1)]
    low = lax.ppermute(strips[0], "lat", forward)
    high = lax.ppermute(strips[1], "lat", [(b, a) for a, b in forward])
    return [low, high]


def taps_body(plan, entries, lift_hbm, place_hbm, weight_hbm, out, *scratch):
    held, sem = scratch[:3], scratch[3]
    copies = [
        pltpu.make_async_copy(source, target, sem.at[order])
        for order, (source, target) in enumerate(zip((lift_hbm, place_hbm, weight_hbm), held))
    ]
    for copy in copies:
        copy.start()
    size, lat_total = lift_hbm.shape
    cols, width = plan.cols, out.shape[2]
    south = is_south(plan)
    row_start = lax.axis_index("lat") * plan.rows
    source_row = lax.broadcasted_iota(jnp.int32, (lat_total, lanes), 0)
    spots = {}
    for span in {plan.taps_size(slot) for slot in range(plan.rows)}:
        spot = lax.broadcasted_iota(jnp.int32, (size, span), 1)
        early = lax.broadcasted_iota(jnp.int32, (size, span), 0) // entries * cols
        spots[span] = lax.rem(spot + early, span)
    tall = size // entries * cols
    basis_row = lax.broadcasted_iota(jnp.int32, (tall, size), 0) // cols
    basis_col = lax.broadcasted_iota(jnp.int32, (tall, size), 1) // entries
    gather = jnp.where(basis_row == basis_col, 1.0, 0.0).astype(jnp.bfloat16)
    for copy in copies:
        copy.wait()
    tables = [ref[...].astype(jnp.bfloat16) for ref in held]
    for slot in range(plan.rows):
        first, count = plan.span(slot)
        center = (plan.half - 1) * cols - first
        here = source_row == row_start + row_of(plan, south, slot + 1)
        here = jnp.where(here, 1.0, 0.0).astype(jnp.bfloat16)
        lift, place, weight = [
            jnp.dot(table, here, preferred_element_type=jnp.float32) for table in tables
        ]
        lift = jnp.where(south, -lift, lift).astype(jnp.int32)
        place = place.astype(jnp.int32) + center
        sources = plan.sources(slot)
        span = plan.taps_size(slot)
        if count == plan.lon_total:
            place = jnp.where(place < 0, place + count, place)
            pieces = [(source - slot - 1, order * count) for order, source in enumerate(sources)]
        else:
            place = place + (lift + slot + 1 - sources[0]) * count
            pieces = [(None, 0)]
        place, weight, lift = [
            jnp.concatenate([v] * (span // lanes), axis=1) for v in (place, weight, lift)
        ]
        part = jnp.where(spots[span] == place, weight, 0.0)
        for offset, start in pieces:
            chosen = part if offset is None else jnp.where(lift == offset, part, 0.0)
            taps = jnp.dot(
                gather, chosen.astype(jnp.bfloat16), preferred_element_type=jnp.float32
            )
            taps = pltpu.roll(taps, 0, 1, stride=1, stride_axis=0)
            out[slot, :, start : start + span] = taps.astype(jnp.bfloat16)


def make_taps(plan, support):
    kinds, _, entries = support[0].shape
    width = max(plan.taps_width(slot) for slot in range(plan.rows))
    tables = [s.transpose(0, 2, 1).reshape(kinds * entries, -1) for s in support]
    scratch = [pltpu.VMEM(t.shape, t.dtype) for t in tables]
    tables = [pltpu.with_memory_space_constraint(t, pltpu.HBM) for t in tables]
    return pl.pallas_call(
        functools.partial(taps_body, plan, entries),
        out_shape=jax.ShapeDtypeStruct((plan.rows, kinds * plan.cols, width), jnp.bfloat16),
        in_specs=[pl.BlockSpec(memory_space=pltpu.HBM)] * 3,
        out_specs=vmem,
        scratch_shapes=scratch + [pltpu.SemaphoreType.DMA((3,))],
        compiler_params=pltpu.CompilerParams(vmem_limit_bytes=8 * mib),
        cost_estimate=pl.CostEstimate(flops=3 * 10**9, bytes_accessed=10**7, transcendentals=0),
        name="filter_taps",
    )(*tables)


def fill_window(plan, sources, south, x_ref, got, edges, win):
    rows, cols = plan.rows, plan.cols
    middle = (plan.half - 1) * cols
    for slot in sources:
        if slot in (0, rows + 1):
            strip = edges[0][...]
            if plan.outer:
                first, last = (edges[1], edges[0]) if slot == 0 else (edges[0], edges[1])
                strip = jnp.where(south, first[...], last[...])
            gap = plan.margin_blocks * cols - plan.margin
            if gap > 0:
                gap = jnp.zeros((gap, strip.shape[1]), strip.dtype)
                strip = jnp.concatenate([gap, strip, gap], axis=0)
            start = middle - plan.margin_blocks * cols
            users = [s for s in range(rows) if slot in plan.sources(s)]
            if max(plan.blocks[s] for s in users) > plan.margin_blocks:
                win[sources.index(slot)] = jnp.zeros(win.shape[1:], win.dtype)
            win[sources.index(slot), start : start + strip.shape[0]] = strip
        else:
            win[sources.index(slot), middle : middle + cols] = x_ref[row_of(plan, south, slot)]
    for (dist, sign), ref in got.items():
        place = middle + sign * dist * cols
        for slot, start, width in plan.moves[dist, sign]:
            if slot not in sources:
                continue
            block = ref[start : start + width]
            if width < cols:
                gap = jnp.zeros((cols - width, block.shape[1]), block.dtype)
                block = jnp.concatenate([block, gap] if sign == 1 else [gap, block], axis=0)
            win[sources.index(slot), place : place + cols] = block


def compute_body(plan, slots, moves, edge_count, chained, *refs):
    x_ref = refs[0]
    got = dict(zip(moves, refs[1:]))
    used = 1 + len(moves)
    edges = refs[used : used + edge_count]
    used += edge_count
    taps_ref, mix_ref, gain_ref, up_ref, down_ref = refs[used : used + 5]
    used += 5 + chained
    out_ref, win, response, result, sem = refs[used:]
    rows, cols = plan.rows, plan.cols
    channels = x_ref.shape[2]
    kinds = mix_ref.shape[0] // channels
    south = is_south(plan)
    middle = (plan.half - 1) * cols
    sources = sorted({s for slot in slots for s in plan.sources(slot)})
    fill_window(plan, sources, south, x_ref, got, edges, win)
    for order, slot in enumerate(slots):
        first, count = plan.span(slot)
        found = [win[sources.index(s), first : first + count] for s in plan.sources(slot)]
        total = jnp.dot(
            taps_ref[slot, :, : count * len(found)],
            jnp.concatenate(found, axis=0),
            preferred_element_type=jnp.float32,
        )
        total = total.astype(jnp.bfloat16)
        for kind in range(kinds):
            place = slice(order * cols, (order + 1) * cols)
            depth = slice(kind * channels, (kind + 1) * channels)
            response[place, depth] = total[kind * cols : (kind + 1) * cols]
    mixed = jnp.dot(response[...], mix_ref[...], preferred_element_type=jnp.float32)
    own = [win[sources.index(slot + 1), middle : middle + cols] for slot in slots]
    latent = jnp.concatenate(own, axis=0).astype(jnp.float32) + mixed
    mean = jnp.mean(latent, axis=1, keepdims=True)
    variance = jnp.mean(jnp.square(latent - mean), axis=1, keepdims=True)
    normed = (latent - mean) * lax.rsqrt(variance + norm_eps) * gain_ref[...]
    hidden = jnp.dot(normed.astype(jnp.bfloat16), up_ref[...], preferred_element_type=jnp.float32)
    hidden = (0.5 * hidden * (1.0 + lax.erf(hidden * 0.5**0.5))).astype(jnp.bfloat16)
    output = latent + jnp.dot(hidden, down_ref[...], preferred_element_type=jnp.float32)
    output = output.astype(jnp.bfloat16)
    copies = []
    for number, (offset, run) in enumerate(runs_of(slots)):
        size = len(run)
        for order in range(size):
            spot = offset + jnp.where(south, size - 1 - order, order)
            place = (offset + order) * cols
            result[spot] = output[place : place + cols]
        first_row = jnp.where(south, rows - 1 - run[-1], run[0])
        source = result.at[pl.ds(offset, size)]
        target = out_ref.at[pl.ds(first_row, size)]
        copies.append(pltpu.make_async_copy(source, target, sem.at[number]))
        copies[-1].start()
    for copy in copies:
        copy.wait()


def runs_of(slots):
    runs = []
    for position, slot in enumerate(slots):
        if runs and runs[-1][1][-1] + 1 == slot:
            runs[-1][1].append(slot)
        else:
            runs.append((position, [slot]))
    return runs


def compute(plan, slots, x, got, edges, taps, weights, chain):
    sources = sorted({s for slot in slots for s in plan.sources(slot)})
    moves = [m for m, picks in plan.moves.items() if any(p[0] in sources for p in picks)]
    reach = max(plan.blocks[slot] for slot in slots)
    moves = [m for m in moves if m[0] <= reach]
    edges = edges if set(sources) & {0, plan.rows + 1} else []
    args = [x, *[got[m] for m in moves], *edges, taps, *weights]
    specs = [vmem] * len(args)
    if chain is not None:
        args.append(chain)
        specs.append(anywhere)
    channels = x.shape[2]
    depth = weights[0].shape[0]
    return pl.pallas_call(
        functools.partial(compute_body, plan, slots, moves, len(edges), chain is not None),
        out_shape=jax.ShapeDtypeStruct(x.shape, x.dtype),
        in_specs=specs,
        out_specs=anywhere,
        scratch_shapes=[
            pltpu.VMEM((len(sources), plan.lon_total, channels), x.dtype),
            pltpu.VMEM((len(slots) * plan.cols, depth), x.dtype),
            pltpu.VMEM((len(slots), plan.cols, channels), x.dtype),
            pltpu.SemaphoreType.DMA((len(runs_of(slots)),)),
        ],
        input_output_aliases={} if chain is None else {len(args) - 1: 0},
        compiler_params=pltpu.CompilerParams(vmem_limit_bytes=24 * mib),
        cost_estimate=pl.CostEstimate(flops=10**6, bytes_accessed=10**5, transcendentals=0),
        name="filter_mix_mlp",
    )(*args)


def on_device(
    fields,
    support_rows,
    support_lons,
    support_weights,
    mix_weight,
    norm_gain,
    up_weight,
    down_weight,
):
    channels, rows, cols = fields.shape
    count = lax.axis_size("lon")
    plan = Plan(rows, cols, lax.axis_size("lat"), count)
    half = plan.half
    x = jnp.transpose(fields, (1, 2, 0))

    direct = [m for m in plan.moves if m[0] < half - 1 or m[0] == half]
    order = [[(1, 1)], [(half, 1)], [(1, -1)]]
    order = [[m for m in group if m in direct] for group in order]
    order.append([m for m in direct if all(m not in group for group in order)])
    sent, later = {}, x
    for group in order:
        if group:
            packed = pack(plan, group, later)
            sent.update(zip(group, packed))
            later, _ = lax.optimization_barrier((later, packed))

    def shifted(value, step):
        return lax.ppermute(value, "lon", [((i + step) % count, i) for i in range(count)])

    got = {m: shifted(sent[m], m[0] * m[1]) for m in direct}
    forward = (half - 1, 1) in plan.moves and half > 2
    if forward:
        got[half - 1, -1] = shifted(got[half, 1], 1)
    taps = make_taps(plan, (support_rows, support_lons, support_weights))
    if forward:
        opposite, taps = lax.optimization_barrier((got[half, 1], taps))
        got[half - 1, 1] = shifted(opposite, -1)
    first = [m for m in got if m[0] <= plan.margin_blocks]
    joined, taps = lax.optimization_barrier(([got[m] for m in first], taps))
    got.update(zip(first, joined))
    edges = edge_rows(plan, x, got)
    weights = (mix_weight.reshape(-1, channels), norm_gain[None], up_weight, down_weight)
    inner = range(1 if plan.outer else 0, rows - 1)
    near = [slot for slot in inner if plan.blocks[slot] <= 1]
    far = [slot for slot in range(rows) if slot not in near]
    output = None
    for slots in (near, far):
        if slots:
            output = compute(plan, slots, x, got, edges, taps, weights, output)
    return jnp.transpose(output, (2, 0, 1))


def solution(mesh):
    in_specs = (P("member", "lat", "lon"), P(), P(), P(), P(), P(), P(), P())
    out_specs = P("member", "lat", "lon")
    return jax.shard_map(
        on_device, mesh=mesh, in_specs=in_specs, out_specs=out_specs, check_vma=False
    )
```
